512 devices in a mesh: leaf: 64 (over x, z), grp: 8 (over y, core).
Axes of the slice: x: 4, y: 4, z: 16, core: 2. Of those that a mesh axis runs over, the one named last changes fastest.
Arguments:
- diag_block: float32 [24576, 384], P(('leaf', 'grp')), as said below
- generator: float32 [24576, 128], P(('leaf', 'grp')), may hold values from -0.3125 to 0.3125
- right_sides: float32 [24576, 1024], P('leaf', 'grp'), may hold values from -6 to 6
- interp_first: float32 [12288, 384], P('leaf'), may hold values from -0.109375 to 0.109375
- interp_second: float32 [6144, 384], P('leaf'), may hold values from -0.109375 to 0.109375
- interp_third: float32 [3072, 384], P('leaf'), may hold values from -0.109375 to 0.109375
- interp_fourth: float32 [1536, 384], P('leaf'), may hold values from -0.109375 to 0.109375
- node_ranks: int32 [64], replicated, may hold values from 128 to 384, as said below
Outputs:
- reduced_block: float32 [24576, 384], P(('leaf', 'grp'))
- reduced_generator: float32 [24576, 128], P(('leaf', 'grp'))
- reduced_rhs: float32 [24576, 1024], P('leaf', 'grp')
The draws below stay inside these ranges and needn't reach their ends.
Inputs may be any that keep to these rules, and one draw needn't show every extreme that they name: Every 384 x 384 block of diag_block is symmetric positive definite with smallest eigenvalue at least 0.002. `node_ranks`: some base node has rank 384 and some has rank 128.
All inputs are finite; a program needn't handle non-finite values.
Results may differ from the reference program's by a relative error of at most 0.0005.
Values sent between devices are 32-bit elements; how exact they have to be, the bound alone decides.
No kernel may reach another device: no remote copies, remote signals or barrier semaphores. Data moves between devices by JAX's collectives and lax.ppermute only.
A program may use at most 64 MiB of HBM per device.

```python
import jax
import jax.numpy as jnp
from jax import lax

R = 384
K = 128
LEVELS = 4
RMIN = 128
BASE_NODES = 64
NRHS = 1024


def draw_diag_block(key, part):
    strong_key = jax.random.fold_in(key, 11)
    weak_key = jax.random.fold_in(key, 12)
    column_count = R // 8
    strong_factor = jax.random.randint(strong_key, (BASE_NODES, R, column_count), -7, 8).astype(jnp.float32)
    weak_factor = jax.random.randint(weak_key, (BASE_NODES, R, R), -7, 8).astype(jnp.float32)
    strong_gram = jnp.einsum('nij,nkj->nik', strong_factor, strong_factor, precision=lax.Precision.HIGHEST)
    weak_gram = jnp.einsum('nij,nkj->nik', weak_factor, weak_factor, precision=lax.Precision.HIGHEST)
    variance = 56.0 / 3.0
    lowest_level = 0.002
    strong_weight = 4.0
    identity = jnp.eye(R, dtype=jnp.float32)
    blocks = lowest_level * identity[None] + weak_gram * (lowest_level / (R * variance)) + strong_gram * (strong_weight / (R * variance))
    return blocks.reshape(BASE_NODES * R, R).astype(jnp.float32)


def draw_node_ranks(key, part):
    values = jax.random.randint(jax.random.fold_in(key, 21), (BASE_NODES,), RMIN, R + 1)
    values = values.at[0].set(R).at[1].set(RMIN)
    return values.astype(jnp.int32)


def level_of(rng, shape, cuts, low, high):
    def one(position, parts):
        steps = jax.random.uniform(jax.random.fold_in(jax.random.fold_in(rng, 6), position), (parts,), jnp.float32, low / len(cuts), high / len(cuts))
        return jnp.repeat(jnp.exp(steps), shape[position] // parts).reshape((-1,) + (1,) * (len(shape) - position - 1))

    level = one(*cuts[0])
    for cut in cuts[1:]:
        level = level * one(*cut)
    return level


def gaussian(rng, shape, width, bound, split=(), kind=jnp.bfloat16):
    gain = level_of(rng, shape, split, -0.22, 0.18) if split else 1.0
    drawn = jax.random.normal(rng, shape, jnp.float32) * width * gain
    return jnp.minimum(jnp.maximum(drawn, -bound), bound).astype(kind)


def setup_inputs(seed: int = 0) -> dict:
    keys = jax.random.split(jax.random.key(seed), 9)
    return {
        "diag_block": draw_diag_block(jax.random.fold_in(keys[8], 71), 0),
        "generator": gaussian(keys[1], (BASE_NODES * R, K), R ** -0.5, 0.3125, ((0, 512),), jnp.float32),
        "right_sides": gaussian(keys[2], (BASE_NODES * R, NRHS), 1.0, 6.0, ((0, 64), (1, 8)), jnp.float32),
        "interp_first": gaussian(keys[3], (BASE_NODES * R // 2, R), (8 * R) ** -0.5, 0.109375, ((0, 64),), jnp.float32),
        "interp_second": gaussian(keys[4], (BASE_NODES * R // 4, R), (8 * R) ** -0.5, 0.109375, ((0, 64),), jnp.float32),
        "interp_third": gaussian(keys[5], (BASE_NODES * R // 8, R), (8 * R) ** -0.5, 0.109375, ((0, 64),), jnp.float32),
        "interp_fourth": gaussian(keys[6], (BASE_NODES * R // 16, R), (8 * R) ** -0.5, 0.109375, ((0, 64),), jnp.float32),
        "node_ranks": draw_node_ranks(jax.random.fold_in(keys[8], 71), 0),
    }


def product(first_factor, second_factor):
    return jnp.dot(first_factor.astype(jnp.float32), second_factor.astype(jnp.float32), precision=lax.Precision.HIGHEST, preferred_element_type=jnp.float32)

def triangle_solve(factor, values):
    return jax.scipy.linalg.solve_triangular(factor, values, lower=True)

def mask_block(diagonal, generator_block, right_block, node_rank):
    row_ids = jnp.arange(diagonal.shape[0])[:, None]
    col_ids = jnp.arange(diagonal.shape[1])[None, :]
    inside_rows = row_ids < node_rank
    identity = jnp.where(row_ids == col_ids, 1.0, 0.0).astype(jnp.float32)
    diagonal = jnp.where(inside_rows & (col_ids < node_rank), diagonal, identity)
    generator_block = jnp.where(inside_rows, generator_block, 0.0)
    right_block = jnp.where(inside_rows, right_block, 0.0)
    return (diagonal, generator_block, right_block)

def merge_pair(low_diag, high_diag, low_gen, high_gen, low_rhs, high_rhs, mixing, low_rank, high_rank):
    row_ids = jnp.arange(mixing.shape[0])[:, None]
    col_ids = jnp.arange(mixing.shape[1])[None, :]
    mixing = jnp.where((row_ids < high_rank) & (col_ids < low_rank), mixing, 0.0)
    low_full = low_diag + product(low_gen, low_gen.T)
    high_full = high_diag + product(high_gen, high_gen.T)
    coupling = product(low_gen, high_gen.T)
    high_mixed = product(high_full, mixing)
    cross = coupling + high_mixed.T
    coupled_mixed = product(low_gen, product(high_gen.T, mixing))
    pivot = low_full + coupled_mixed + coupled_mixed.T + product(mixing.T, high_mixed)
    factor = jnp.linalg.cholesky(pivot)
    solved = triangle_solve(factor, cross)
    reduced = high_full - product(solved.T, solved)
    gen_input = low_gen + product(mixing.T, high_gen)
    new_gen = high_gen - product(solved.T, triangle_solve(factor, gen_input))
    rhs_input = low_rhs + product(mixing.T, high_rhs)
    new_rhs = high_rhs - product(solved.T, triangle_solve(factor, rhs_input))
    return (reduced, new_gen, new_rhs)

def reference(diag_block, generator, right_sides, interp_first, interp_second, interp_third, interp_fourth, node_ranks):
    node_count = diag_block.shape[0] // R
    diagonals = diag_block.reshape(node_count, R, R)
    generators = generator.reshape(node_count, R, K)
    rhs_blocks = right_sides.reshape(node_count, R, -1)
    diagonals, generators, rhs_blocks = jax.vmap(mask_block)(diagonals, generators, rhs_blocks, node_ranks)
    mixings = (interp_first, interp_second, interp_third, interp_fourth)
    for height in range(LEVELS):
        span_size = 2 ** height
        level_ranks = node_ranks.reshape(-1, span_size)[:, -1]
        mixing_blocks = mixings[height].reshape(-1, R, R)
        diagonals, generators, rhs_blocks = jax.vmap(merge_pair)(diagonals[0::2], diagonals[1::2], generators[0::2], generators[1::2], rhs_blocks[0::2], rhs_blocks[1::2], mixing_blocks, level_ranks[0::2], level_ranks[1::2])
    spread = 2 ** LEVELS
    out_block = jnp.repeat(diagonals, spread, axis=0).reshape(-1, R)
    out_gen = jnp.repeat(generators, spread, axis=0).reshape(-1, K)
    out_rhs = jnp.repeat(rhs_blocks, spread, axis=0).reshape(node_count * R, -1)
    return (out_block, out_gen, out_rhs)
```

```python
import functools

import jax
import jax.numpy as jnp
from jax import lax
from jax.experimental import pallas as pl
from jax.experimental.pallas import tpu as pltpu
from jax.sharding import Mesh, PartitionSpec as P

LEVELS = 4
N = 384
K = 128
T = 128
W = 16
SHARE = 48
PACK = 64
LEAF = ("x", "z3", "z2", "z1", "z0")
GRP = ("y", "c")
MIXED = (24, 16, 8, 8)
HIGHEST = lax.Precision.HIGHEST
VMEM = pl.BlockSpec(memory_space=pltpu.VMEM)
SMEM = pl.BlockSpec(memory_space=pltpu.SMEM)


def dot(first, second, first_axis=1, second_axis=0):
    return lax.dot_general(
        first,
        second,
        (((first_axis,), (second_axis,)), ((), ())),
        precision=HIGHEST,
        preferred_element_type=jnp.float32,
    )


def wide(values):
    return jnp.broadcast_to(values, (8, T))


def sweep_panel(rows, start):
    lanes = lax.broadcasted_iota(jnp.int32, (8, T), 1)
    subs = lax.broadcasted_iota(jnp.int32, (8, T), 0)
    cols = [[wide(part[:, start + m : start + m + 1]) for part in rows] for m in range(W)]
    factor = [jnp.zeros((8, T), jnp.float32) for _ in rows]
    for k in range(W):
        group, sub = divmod(k, 8)
        here = subs == sub
        pivot = wide(cols[k][group][sub : sub + 1, :])
        inverse = 1.0 / pivot
        mult = list(cols[k])
        mult[group] = jnp.where(here, -1.0, mult[group])
        for m in range(k + 1, W):
            step = wide(cols[m][group][sub : sub + 1, :]) * inverse
            kept = list(cols[m])
            kept[group] = jnp.where(here, 0.0, kept[group])
            cols[m] = [part - q * step for part, q in zip(kept, mult)]
        lane = lanes == start + k
        row = jnp.where(lane, 1.0, wide(rows[group][sub : sub + 1, :]))
        scaled = jnp.where(lanes <= start + k, row, 0.0) * lax.rsqrt(pivot)
        factor[group] = jnp.where(here, scaled, factor[group])
        step = row * inverse
        kept = [jnp.where(lane | here if i == group else lane, 0.0, part) for i, part in enumerate(rows)]
        rows = [part - q * step for part, q in zip(kept, mult)]
    return rows, factor


def inverse_factor(block):
    lanes = lax.broadcasted_iota(jnp.int32, (8, T), 1)
    rows = [block[8 * i : 8 * i + 8, :] for i in range(W // 8)]
    below = block[W:]
    out = []
    for start in range(0, T, W):
        swept, factor = sweep_panel(rows, start)
        out += factor
        if start + W == T:
            break
        panel = jnp.concatenate(swept, axis=0)
        inside = (lanes >= start) & (lanes < start + W)
        rows = []
        for i in range(W // 8):
            part = below[8 * i : 8 * i + 8, :]
            total = jnp.where(inside, 0.0, part)
            for k in range(W):
                total = total - wide(part[:, start + k : start + k + 1]) * wide(panel[k : k + 1, :])
            rows.append(total)
        if start + 2 * W < T:
            below = below[W:]
            drop = dot(below[:, start : start + W], panel)
            span = lax.broadcasted_iota(jnp.int32, below.shape, 1)
            below = jnp.where((span >= start) & (span < start + W), 0.0, below) - drop
    return jnp.concatenate(out, axis=0)


def unpack(gathered, first):
    order = [(g % 2, g // 2) for g in range(8)]
    block = jnp.concatenate([gathered[c, y, first : first + SHARE, :] for c, y in order], axis=0)
    third = SHARE // 3
    gen = jnp.concatenate(
        [
            gathered[c, y, first + SHARE : first + PACK, K * q : K * (q + 1)]
            for c, y in order
            for q in range(3)
        ],
        axis=0,
    )
    assert third * 3 == SHARE
    return block, gen


def unpack_mixing(gathered, first, height):
    order = [(g % 2, g // 2) for g in range(8)]
    piece = N >> height + 1
    rows = MIXED[height]
    tiles = []
    for sub in range(2 << height):
        for part in range(piece // rows):
            member, slot = part, sub
            if height == 3 and sub >= 8:
                member, slot = part + 3, sub - 8
            c, y = order[member]
            at = first + slot * rows
            tiles.append(gathered[c, y, at : at + rows, :])
    return jnp.concatenate(tiles, axis=0)


def masked(block, gen, rank):
    rows = lax.broadcasted_iota(jnp.int32, (N, N), 0)
    cols = lax.broadcasted_iota(jnp.int32, (N, N), 1)
    identity = jnp.where(rows == cols, 1.0, 0.0)
    block = jnp.where((rows < rank) & (cols < rank), block, identity)
    inside = lax.broadcasted_iota(jnp.int32, (N, K), 0) < rank
    return block, jnp.where(inside, gen, 0.0)


def merge_kernel(height, place, ranks, gathered, *refs):
    last = height == LEVELS - 1
    leaf, member = place[0], place[1]
    base = leaf >> height + 1 << height + 1
    low_rank = ranks[base + 2**height - 1]
    high_rank = ranks[base + 2 ** (height + 1) - 1]
    upper = leaf >> height & 1 == 1
    if height == 0:
        own_block, own_gen = unpack(gathered, 0)
        peer_block, peer_gen = unpack(gathered, PACK)
        first = 2 * PACK
        outs = refs
    else:
        own_block, own_gen = refs[0][...], refs[1][...]
        peer_block, peer_gen = unpack(gathered, 0)
        first = PACK
        outs = refs[2:]
    low_block = jnp.where(upper, peer_block, own_block)
    high_block = jnp.where(upper, own_block, peer_block)
    low_gen = jnp.where(upper, peer_gen, own_gen)
    high_gen = jnp.where(upper, own_gen, peer_gen)
    if height == 0:
        low_block, low_gen = masked(low_block, low_gen, low_rank)
        high_block, high_gen = masked(high_block, high_gen, high_rank)
    rows = lax.broadcasted_iota(jnp.int32, (N, N), 0)
    cols = lax.broadcasted_iota(jnp.int32, (N, N), 1)
    inside = (rows < high_rank) & (cols < low_rank)
    mixing = jnp.where(inside, unpack_mixing(gathered, first, height), 0.0)

    high_mixed = dot(high_block, mixing)
    gen_input = low_gen + dot(mixing, high_gen, 0, 0)
    pivot = low_block + dot(gen_input, gen_input, 1, 1) + dot(mixing, high_mixed, 0, 0)
    cross = dot(gen_input, high_gen, 1, 1) + high_mixed.T
    rest = jnp.concatenate([pivot, cross, gen_input], axis=1)
    solved, solved_gen, above, inverses = [], [], [], []
    for i in range(N // T):
        inverse = inverse_factor(rest[:T, :T])
        inverses.append(inverse)
        done = dot(inverse, rest[:T, T:])
        left = N - T * (i + 1)
        solved.append(done[:, left : left + N])
        solved_gen.append(done[:, left + N :])
        if left:
            above.append(done[:, :left])
            rest = rest[T:, T:] - dot(done[:, :left], done, 0, 0)
    solved = jnp.concatenate(solved, axis=0)
    solved_gen = jnp.concatenate(solved_gen, axis=0)
    block = high_block + dot(high_gen, high_gen, 1, 1) - dot(solved, solved, 0, 0)
    gen = high_gen - dot(solved, solved_gen, 0, 0)

    solved_ref, inverse_ref, above_ref, mixing_ref = outs[:4]
    solved_ref[...] = solved
    inverse_ref[...] = jnp.concatenate(inverses, axis=1)
    above_ref[...] = jnp.concatenate(above, axis=1)
    mixing_ref[...] = mixing
    own = pl.ds(pl.multiple_of(member * SHARE, 8), SHARE)
    block_ref, gen_ref = outs[4], outs[5]
    if last:
        keep_block, keep_gen = outs[6], outs[7]
        keep_block[...] = block
        keep_gen[...] = gen
        block_ref[...] = keep_block[own, :]
        gen_ref[...] = keep_gen[own, :]
    else:
        block_ref[...] = block
        gen_ref[...] = gen
        share_ref = outs[6]
        share_ref[:SHARE, :] = block_ref[own, :]
        third = SHARE // 3
        for q in range(3):
            at = pl.ds(pl.multiple_of(member * SHARE + q * third, 8), third)
            share_ref[SHARE:, K * q : K * (q + 1)] = gen_ref[at, :]


def merge(height, place, ranks, gathered, *own):
    last = height == LEVELS - 1
    shapes = [(N, N), (T, N), (T, N), (N, N)]
    shapes += [(SHARE, N), (SHARE, K)] if last else [(N, N), (N, K), (PACK, N)]
    return pl.pallas_call(
        functools.partial(merge_kernel, height),
        out_shape=[jax.ShapeDtypeStruct(shape, jnp.float32) for shape in shapes],
        in_specs=[SMEM, SMEM] + [VMEM] * (1 + len(own)),
        out_specs=[VMEM] * len(shapes),
        scratch_shapes=[pltpu.VMEM((N, N), jnp.float32), pltpu.VMEM((N, K), jnp.float32)] if last else [],
        compiler_params=pltpu.CompilerParams(vmem_limit_bytes=40 * 2**20),
        name="merge%d" % height,
    )(place, ranks, gathered, *own)


def rhs_kernel(height, place, ranks, solved, inverses, above, mixing, own, peer, out):
    leaf = place[0]
    upper = leaf >> height & 1 == 1
    low = jnp.where(upper, peer[...], own[...])
    high = jnp.where(upper, own[...], peer[...])
    if height == 0:
        base = leaf >> 1 << 1
        rows = lax.broadcasted_iota(jnp.int32, low.shape, 0)
        low = jnp.where(rows < ranks[base], low, 0.0)
        high = jnp.where(rows < ranks[base + 1], high, 0.0)
    rest = low + dot(mixing[...], high, 0, 0)
    done = []
    at = 0
    for i in range(N // T):
        done.append(dot(inverses[:, T * i : T * (i + 1)], rest[:T]))
        left = N - T * (i + 1)
        if left:
            rest = rest[T:] - dot(above[:, at : at + left], done[-1], 0, 0)
            at += left
    out[...] = high - dot(solved[...], jnp.concatenate(done, axis=0), 0, 0)


def merge_rhs(height, place, ranks, solved, inverses, above, mixing, own, peer):
    return pl.pallas_call(
        functools.partial(rhs_kernel, height),
        out_shape=jax.ShapeDtypeStruct(own.shape, jnp.float32),
        in_specs=[SMEM, SMEM] + [VMEM] * 6,
        out_specs=VMEM,
        compiler_params=pltpu.CompilerParams(vmem_limit_bytes=24 * 2**20),
        name="rhs%d" % height,
    )(place, ranks, solved, inverses, above, mixing, own, peer)


def swapped(block, bit):
    return lax.ppermute(block, "z%d" % bit, [(0, 1), (1, 0)])


def joined(own, peer, bit):
    upper = lax.axis_index("z%d" % bit) == 1
    return jnp.where(upper, jnp.concatenate([peer, own]), jnp.concatenate([own, peer]))


def spread(share):
    return lax.all_gather(lax.all_gather(share, "y", axis=0), "c", axis=0)


def on_device(diag_block, generator, right_sides, *rest):
    pieces, node_ranks = rest[:LEVELS], rest[LEVELS]
    leaf = lax.axis_index(LEAF)
    member = lax.axis_index(GRP)
    place = jnp.where(jnp.arange(2) == 0, leaf, member).astype(jnp.int32)
    third = SHARE // 3
    packed_gen = jnp.concatenate([generator[third * q : third * (q + 1)] for q in range(3)], axis=1)
    share = jnp.concatenate([diag_block, packed_gen], axis=0)
    tiles = []
    for height, piece in enumerate(pieces):
        count = piece.shape[0] // MIXED[height]
        at = member % count * MIXED[height]
        tiles.append(lax.dynamic_slice_in_dim(piece, at, MIXED[height], 0))
    received = swapped(jnp.concatenate([share] + tiles, axis=0), 0)
    offset = PACK
    for height in range(LEVELS):
        peer = received[offset : offset + MIXED[height]]
        offset += MIXED[height]
        tiles[height] = joined(tiles[height], peer, 0)
    peer_share = received[:PACK]
    right_sides, peer_share = lax.optimization_barrier((right_sides, peer_share))
    peer_rhs = swapped(right_sides, 0)
    for bit in (1, 2):
        stacked = swapped(jnp.concatenate(tiles[bit:], axis=0), bit)
        offset = 0
        for height in range(bit, LEVELS):
            count = tiles[height].shape[0]
            tiles[height] = joined(tiles[height], stacked[offset : offset + count], bit)
            offset += count
    far = swapped(tiles[3], 3)
    tiles[3] = jnp.where((lax.axis_index("z3") == 1) == (member >= 3), tiles[3], far)

    gathered = spread(jnp.concatenate([share, peer_share, tiles[0]], axis=0))
    rhs_now = right_sides
    own = ()
    for height in range(LEVELS):
        made = merge(height, place, node_ranks, gathered, *own)
        factors, own = made[:4], made[4:6]
        if height == LEVELS - 1:
            rhs_now = merge_rhs(height, place, node_ranks, *factors, rhs_now, peer_rhs)
            break
        peer_share = swapped(made[6], height + 1)
        rhs_now = merge_rhs(height, place, node_ranks, *factors, rhs_now, peer_rhs)
        peer_rhs = swapped(rhs_now, height + 1)
        gathered = spread(jnp.concatenate([peer_share, tiles[height + 1]], axis=0))
    return (own[0], own[1], rhs_now)


def solution(mesh):
    fine = Mesh(mesh.devices.reshape(4, 2, 2, 2, 2, 4, 2), LEAF + GRP)
    rows = P(LEAF + GRP, None)
    leaves = P(LEAF, None)
    columns = P(LEAF, GRP)
    return jax.shard_map(
        on_device,
        mesh=fine,
        in_specs=(rows, rows, columns, leaves, leaves, leaves, leaves, P()),
        out_specs=(rows, rows, columns),
        check_vma=False,
    )
```

```python
import functools

import jax
import jax.numpy as jnp
from jax import lax
from jax.experimental import pallas as pl
from jax.experimental.pallas import tpu as pltpu
from jax.sharding import Mesh, PartitionSpec as P

LEVELS = 4
N = 384
K = 128
T = 128
W = 16
SHARE = 48
PACK = 64
LEAF = ("x", "z3", "z2", "z1", "z0")
GRP = ("y", "c")
Z = ("z3", "z2", "z1", "z0")
MIXED = (96, 24, 16, 8)
HIGHEST = lax.Precision.HIGHEST
VMEM = pl.BlockSpec(memory_space=pltpu.VMEM)
SMEM = pl.BlockSpec(memory_space=pltpu.SMEM)


def dot(first, second, first_axis=1, second_axis=0):
    return lax.dot_general(
        first,
        second,
        (((first_axis,), (second_axis,)), ((), ())),
        precision=HIGHEST,
        preferred_element_type=jnp.float32,
    )


def wide(values):
    return jnp.broadcast_to(values, (8, T))


def sweep_panel(rows, start):
    lanes = lax.broadcasted_iota(jnp.int32, (8, T), 1)
    subs = lax.broadcasted_iota(jnp.int32, (8, T), 0)
    cols = [[wide(part[:, start + m : start + m + 1]) for part in rows] for m in range(W)]
    factor = [jnp.zeros((8, T), jnp.float32) for _ in rows]
    for k in range(W):
        group, sub = divmod(k, 8)
        here = subs == sub
        pivot = wide(cols[k][group][sub : sub + 1, :])
        inverse = 1.0 / pivot
        mult = list(cols[k])
        mult[group] = jnp.where(here, -1.0, mult[group])
        for m in range(k + 1, W):
            step = wide(cols[m][group][sub : sub + 1, :]) * inverse
            kept = list(cols[m])
            kept[group] = jnp.where(here, 0.0, kept[group])
            cols[m] = [part - q * step for part, q in zip(kept, mult)]
        lane = lanes == start + k
        row = jnp.where(lane, 1.0, wide(rows[group][sub : sub + 1, :]))
        scaled = jnp.where(lanes <= start + k, row, 0.0) * lax.rsqrt(pivot)
        factor[group] = jnp.where(here, scaled, factor[group])
        step = row * inverse
        kept = [jnp.where(lane | here if i == group else lane, 0.0, part) for i, part in enumerate(rows)]
        rows = [part - q * step for part, q in zip(kept, mult)]
    return rows, factor


def inverse_factor(block):
    lanes = lax.broadcasted_iota(jnp.int32, (8, T), 1)
    rows = [block[8 * i : 8 * i + 8, :] for i in range(W // 8)]
    below = block[W:]
    out = []
    for start in range(0, T, W):
        swept, factor = sweep_panel(rows, start)
        out += factor
        if start + W == T:
            break
        panel = jnp.concatenate(swept, axis=0)
        inside = (lanes >= start) & (lanes < start + W)
        rows = []
        for i in range(W // 8):
            part = below[8 * i : 8 * i + 8, :]
            total = jnp.where(inside, 0.0, part)
            for k in range(W):
                total = total - wide(part[:, start + k : start + k + 1]) * wide(panel[k : k + 1, :])
            rows.append(total)
        if start + 2 * W < T:
            below = below[W:]
            drop = dot(below[:, start : start + W], panel)
            span = lax.broadcasted_iota(jnp.int32, below.shape, 1)
            below = jnp.where((span >= start) & (span < start + W), 0.0, below) - drop
    return jnp.concatenate(out, axis=0)


def unpack(gathered):
    block = jnp.concatenate([gathered[g, :SHARE, :] for g in range(8)], axis=0)
    gen = jnp.concatenate(
        [gathered[g, SHARE:PACK, K * q : K * (q + 1)] for g in range(8) for q in range(3)], axis=0
    )
    return block, gen


def unpack_first(upper, core, own, near, far):
    even = core == 0
    peer = [jnp.where(even, near[...], far[...]), jnp.where(even, far[...], near[...])]
    peer = jnp.concatenate(peer, axis=0)
    return jnp.concatenate([jnp.where(upper, peer, own[...]), jnp.where(upper, own[...], peer)], axis=0)


def unpack_mixing(height, row, core, own, near, far):
    count = own.shape[0]
    front, even = row == 0, core == 0
    own, near, close, apart = own[...], near[...], far[:count, :], far[count:, :]
    mine = [jnp.where(front, own, near), jnp.where(front, near, own)]
    theirs = [jnp.where(front, close, apart), jnp.where(front, apart, close)]
    parts = []
    for first, second in zip(mine, theirs):
        parts += [jnp.where(even, first, second), jnp.where(even, second, first)]
    rows = MIXED[height]
    tiles = []
    for sub in range(2 << height):
        for part in range((N >> height + 1) // rows):
            tiles.append(parts[part][sub * rows : (sub + 1) * rows, :])
    return jnp.concatenate(tiles, axis=0)


def masked(block, gen, rank):
    rows = lax.broadcasted_iota(jnp.int32, (N, N), 0)
    cols = lax.broadcasted_iota(jnp.int32, (N, N), 1)
    identity = jnp.where(rows == cols, 1.0, 0.0)
    block = jnp.where((rows < rank) & (cols < rank), block, identity)
    inside = lax.broadcasted_iota(jnp.int32, (N, K), 0) < rank
    return block, jnp.where(inside, gen, 0.0)


def merge_kernel(height, place, ranks, gathered, mixing_own, mixing_near, mixing_far, *refs):
    last = height == LEVELS - 1
    leaf, member = place[0], place[1]
    base = leaf >> height + 1 << height + 1
    low_rank = ranks[base + 2**height - 1]
    high_rank = ranks[base + 2 ** (height + 1) - 1]
    upper = leaf >> height & 1 == 1
    peer_block, peer_gen = unpack(gathered)
    if height == 0:
        own_block, own_gen = unpack(refs[0])
        outs = refs[1:]
        mixing = unpack_first(upper, member & 1, mixing_own, mixing_near, mixing_far)
    else:
        own_block, own_gen = refs[0][...], refs[1][...]
        outs = refs[2:]
        mixing = unpack_mixing(height, member >> 1 & 1, member & 1, mixing_own, mixing_near, mixing_far)
    low_block = jnp.where(upper, peer_block, own_block)
    high_block = jnp.where(upper, own_block, peer_block)
    low_gen = jnp.where(upper, peer_gen, own_gen)
    high_gen = jnp.where(upper, own_gen, peer_gen)
    if height == 0:
        low_block, low_gen = masked(low_block, low_gen, low_rank)
        high_block, high_gen = masked(high_block, high_gen, high_rank)
    rows = lax.broadcasted_iota(jnp.int32, (N, N), 0)
    cols = lax.broadcasted_iota(jnp.int32, (N, N), 1)
    inside = (rows < high_rank) & (cols < low_rank)
    mixing = jnp.where(inside, mixing, 0.0)

    high_mixed = dot(high_block, mixing)
    gen_input = low_gen + dot(mixing, high_gen, 0, 0)
    pivot = low_block + dot(gen_input, gen_input, 1, 1) + dot(mixing, high_mixed, 0, 0)
    cross = dot(gen_input, high_gen, 1, 1) + high_mixed.T
    rest = jnp.concatenate([pivot, cross, gen_input], axis=1)
    solved, solved_gen, above, inverses = [], [], [], []
    for i in range(N // T):
        inverse = inverse_factor(rest[:T, :T])
        inverses.append(inverse)
        done = dot(inverse, rest[:T, T:])
        left = N - T * (i + 1)
        solved.append(done[:, left : left + N])
        solved_gen.append(done[:, left + N :])
        if left:
            above.append(done[:, :left])
            rest = rest[T:, T:] - dot(done[:, :left], done, 0, 0)
    solved = jnp.concatenate(solved, axis=0)
    solved_gen = jnp.concatenate(solved_gen, axis=0)
    block = high_block + dot(high_gen, high_gen, 1, 1) - dot(solved, solved, 0, 0)
    gen = high_gen - dot(solved, solved_gen, 0, 0)

    solved_ref, inverse_ref, above_ref, mixing_ref = outs[:4]
    solved_ref[...] = solved
    inverse_ref[...] = jnp.concatenate(inverses, axis=1)
    above_ref[...] = jnp.concatenate(above, axis=1)
    mixing_ref[...] = mixing
    own = pl.ds(pl.multiple_of(member * SHARE, 8), SHARE)
    block_ref, gen_ref = outs[4], outs[5]
    if last:
        keep_block, keep_gen = outs[6], outs[7]
        keep_block[...] = block
        keep_gen[...] = gen
        block_ref[...] = keep_block[own, :]
        gen_ref[...] = keep_gen[own, :]
    else:
        block_ref[...] = block
        gen_ref[...] = gen
        share_ref = outs[6]
        share_ref[:SHARE, :] = block_ref[own, :]
        third = SHARE // 3
        for q in range(3):
            at = pl.ds(pl.multiple_of(member * SHARE + q * third, 8), third)
            share_ref[SHARE:, K * q : K * (q + 1)] = gen_ref[at, :]


def merge(height, place, ranks, gathered, mixing, own):
    last = height == LEVELS - 1
    shapes = [(N, N), (T, N), (T, N), (N, N)]
    shapes += [(SHARE, N), (SHARE, K)] if last else [(N, N), (N, K), (PACK, N)]
    return pl.pallas_call(
        functools.partial(merge_kernel, height),
        out_shape=[jax.ShapeDtypeStruct(shape, jnp.float32) for shape in shapes],
        in_specs=[SMEM, SMEM] + [VMEM] * (4 + len(own)),
        out_specs=[VMEM] * len(shapes),
        scratch_shapes=[pltpu.VMEM((N, N), jnp.float32), pltpu.VMEM((N, K), jnp.float32)] if last else [],
        compiler_params=pltpu.CompilerParams(vmem_limit_bytes=40 * 2**20),
        cost_estimate=pl.CostEstimate(flops=2 * 10**10, transcendentals=0, bytes_accessed=8 * 10**6),
        name="merge%d" % height,
    )(place, ranks, gathered, *mixing, *own)


def rhs_kernel(height, place, ranks, solved, inverses, above, mixing, own, peer, out):
    leaf = place[0]
    upper = leaf >> height & 1 == 1
    low = jnp.where(upper, peer[...], own[...])
    high = jnp.where(upper, own[...], peer[...])
    if height == 0:
        base = leaf >> 1 << 1
        rows = lax.broadcasted_iota(jnp.int32, low.shape, 0)
        low = jnp.where(rows < ranks[base], low, 0.0)
        high = jnp.where(rows < ranks[base + 1], high, 0.0)
    rest = low + dot(mixing[...], high, 0, 0)
    done = []
    at = 0
    for i in range(N // T):
        done.append(dot(inverses[:, T * i : T * (i + 1)], rest[:T]))
        left = N - T * (i + 1)
        if left:
            rest = rest[T:] - dot(above[:, at : at + left], done[-1], 0, 0)
            at += left
    out[...] = high - dot(solved[...], jnp.concatenate(done, axis=0), 0, 0)


def merge_rhs(height, place, ranks, solved, inverses, above, mixing, own, peer):
    return pl.pallas_call(
        functools.partial(rhs_kernel, height),
        out_shape=jax.ShapeDtypeStruct(own.shape, jnp.float32),
        in_specs=[SMEM, SMEM] + [VMEM] * 6,
        out_specs=VMEM,
        compiler_params=pltpu.CompilerParams(vmem_limit_bytes=24 * 2**20),
        cost_estimate=pl.CostEstimate(flops=3 * 10**9, transcendentals=0, bytes_accessed=3 * 10**6),
        name="rhs%d" % height,
    )(place, ranks, solved, inverses, above, mixing, own, peer)


def swapped(block, bit):
    route = []
    for low in range(16):
        if bit < 3:
            high = low ^ 1 << bit
        else:
            high = (low + 4 if low >> 2 & 1 else low - 4) % 16
        route.append((low, high))
    return lax.ppermute(block, Z, route)


def joined(own, peer, bit):
    upper = lax.axis_index("z%d" % bit) == 1
    return jnp.where(upper, jnp.concatenate([peer, own]), jnp.concatenate([own, peer]))


def across_core(block):
    return lax.ppermute(block, "c", [(0, 1), (1, 0)])


def across_chip(block):
    return lax.ppermute(block, "y", [(0, 1), (1, 0), (2, 3), (3, 2)])


def spread(share):
    return lax.all_gather(share, GRP, axis=0)


def on_device(diag_block, generator, right_sides, *rest):
    pieces, node_ranks = rest[:LEVELS], rest[LEVELS]
    leaf = lax.axis_index(LEAF)
    member = lax.axis_index(GRP)
    core = lax.axis_index("c")
    quarter = 2 * (lax.axis_index("y") & 1) + core
    place = jnp.where(jnp.arange(2) == 0, leaf, member).astype(jnp.int32)
    third = SHARE // 3
    packed_gen = jnp.concatenate([generator[third * q : third * (q + 1)] for q in range(3)], axis=1)
    share = jnp.concatenate([diag_block, packed_gen], axis=0)
    tiles = []
    for height, piece in enumerate(pieces):
        count = piece.shape[0] // MIXED[height]
        at = (quarter if height else core) % count * MIXED[height]
        tiles.append(lax.dynamic_slice_in_dim(piece, at, MIXED[height], 0))

    def step(bit, start):
        moved = tiles[start:]
        received = swapped(jnp.concatenate(moved, axis=0), bit)
        offset = 0
        for height, tile in zip(range(start, LEVELS), moved):
            count = tile.shape[0]
            tiles[height] = joined(tile, received[offset : offset + count], bit)
            offset += count

    peer_share = swapped(share, 0)
    near = swapped(tiles[0], 0)
    own_all = spread(share)
    peer_share, near, own_all = lax.optimization_barrier((peer_share, near, own_all))
    mixing = (pieces[0], near, across_core(near))
    step(0, 1)
    gathered = spread(peer_share)
    gathered, tiles[1], tiles[2], tiles[3] = lax.optimization_barrier((gathered, *tiles[1:]))
    step(1, 1)
    rhs_now = right_sides
    peer_rhs = swapped(rhs_now, 0)
    own = (own_all,)
    for height in range(LEVELS):
        made = merge(height, place, node_ranks, gathered, mixing, own)
        factors, own = made[:4], made[4:6]
        if height == LEVELS - 1:
            rhs_now = merge_rhs(height, place, node_ranks, *factors, rhs_now, peer_rhs)
            break
        share, *tiles[height + 1 :] = lax.optimization_barrier((made[6], *tiles[height + 1 :]))
        peer_share = swapped(share, height + 1)
        tile = tiles[height + 1]
        near = across_chip(tile)
        mixing = (tile, near, across_core(jnp.concatenate([tile, near], axis=0)))
        rhs_now = merge_rhs(height, place, node_ranks, *factors, rhs_now, peer_rhs)
        peer_share, rhs_now = lax.optimization_barrier((peer_share, rhs_now))
        peer_rhs = swapped(rhs_now, height + 1)
        if height + 2 < LEVELS:
            step(height + 2, height + 2)
        gathered = spread(peer_share)
    return (own[0], own[1], rhs_now)


def solution(mesh):
    fine = Mesh(mesh.devices.reshape(4, 2, 2, 2, 2, 4, 2), LEAF + GRP)
    rows = P(LEAF + GRP, None)
    leaves = P(LEAF, None)
    columns = P(LEAF, GRP)
    return jax.shard_map(
        on_device,
        mesh=fine,
        in_specs=(rows, rows, columns, leaves, leaves, leaves, leaves, P()),
        out_specs=(rows, rows, columns),
        check_vma=False,
    )
```

```python
import functools

import jax
import jax.numpy as jnp
from jax import lax
from jax.experimental import pallas as pl
from jax.experimental.pallas import tpu as pltpu
from jax.sharding import Mesh, PartitionSpec as P

LEVELS = 4
N = 384
K = 128
T = 128
W = 16
SHARE = 48
PACK = 64
LEAF = ("x", "z3", "z2", "z1", "z0")
GRP = ("y", "c")
Z = ("z3", "z2", "z1", "z0")
MIXED = (96, 24, 16, 8)
HIGHEST = lax.Precision.HIGHEST
VMEM = pl.BlockSpec(memory_space=pltpu.VMEM)
SMEM = pl.BlockSpec(memory_space=pltpu.SMEM)


def dot(first, second, first_axis=1, second_axis=0):
    return lax.dot_general(
        first,
        second,
        (((first_axis,), (second_axis,)), ((), ())),
        precision=HIGHEST,
        preferred_element_type=jnp.float32,
    )


def wide(values):
    return jnp.broadcast_to(values, (8, T))


def sweep_panel(rows, start):
    lanes = lax.broadcasted_iota(jnp.int32, (8, T), 1)
    subs = lax.broadcasted_iota(jnp.int32, (8, T), 0)
    cols = [[wide(part[:, start + m : start + m + 1]) for part in rows] for m in range(W)]
    factor = [jnp.zeros((8, T), jnp.float32) for _ in rows]
    for k in range(W):
        group, sub = divmod(k, 8)
        here = subs == sub
        pivot = wide(cols[k][group][sub : sub + 1, :])
        inverse = 1.0 / pivot
        mult = list(cols[k])
        mult[group] = jnp.where(here, -1.0, mult[group])
        for m in range(k + 1, W):
            step = wide(cols[m][group][sub : sub + 1, :]) * inverse
            kept = list(cols[m])
            kept[group] = jnp.where(here, 0.0, kept[group])
            cols[m] = [part - q * step for part, q in zip(kept, mult)]
        lane = lanes == start + k
        row = jnp.where(lane, 1.0, wide(rows[group][sub : sub + 1, :]))
        scaled = jnp.where(lanes <= start + k, row, 0.0) * lax.rsqrt(pivot)
        factor[group] = jnp.where(here, scaled, factor[group])
        step = row * inverse
        kept = [jnp.where(lane | here if i == group else lane, 0.0, part) for i, part in enumerate(rows)]
        rows = [part - q * step for part, q in zip(kept, mult)]
    return rows, factor


def inverse_factor(block):
    lanes = lax.broadcasted_iota(jnp.int32, (8, T), 1)
    rows = [block[8 * i : 8 * i + 8, :] for i in range(W // 8)]
    below = block[W:]
    out = []
    for start in range(0, T, W):
        swept, factor = sweep_panel(rows, start)
        out += factor
        if start + W == T:
            break
        panel = jnp.concatenate(swept, axis=0)
        inside = (lanes >= start) & (lanes < start + W)
        rows = []
        for i in range(W // 8):
            part = below[8 * i : 8 * i + 8, :]
            total = jnp.where(inside, 0.0, part)
            for k in range(W):
                total = total - wide(part[:, start + k : start + k + 1]) * wide(panel[k : k + 1, :])
            rows.append(total)
        if start + 2 * W < T:
            below = below[W:]
            drop = dot(below[:, start : start + W], panel)
            span = lax.broadcasted_iota(jnp.int32, below.shape, 1)
            below = jnp.where((span >= start) & (span < start + W), 0.0, below) - drop
    return jnp.concatenate(out, axis=0)


def unpack(gathered):
    block = jnp.concatenate([gathered[g, :SHARE, :] for g in range(8)], axis=0)
    gen = jnp.concatenate(
        [gathered[g, SHARE:PACK, K * q : K * (q + 1)] for g in range(8) for q in range(3)], axis=0
    )
    return block, gen


def unpack_first(upper, core, own, near, far):
    even = core == 0
    peer = [jnp.where(even, near[...], far[...]), jnp.where(even, far[...], near[...])]
    peer = jnp.concatenate(peer, axis=0)
    return jnp.concatenate([jnp.where(upper, peer, own[...]), jnp.where(upper, own[...], peer)], axis=0)


def unpack_mixing(height, row, core, own, near, far):
    count = own.shape[0]
    front, even = row == 0, core == 0
    own, near, close, apart = own[...], near[...], far[:count, :], far[count:, :]
    mine = [jnp.where(front, own, near), jnp.where(front, near, own)]
    theirs = [jnp.where(front, close, apart), jnp.where(front, apart, close)]
    parts = []
    for first, second in zip(mine, theirs):
        parts += [jnp.where(even, first, second), jnp.where(even, second, first)]
    rows = MIXED[height]
    tiles = []
    for sub in range(2 << height):
        for part in range((N >> height + 1) // rows):
            tiles.append(parts[part][sub * rows : (sub + 1) * rows, :])
    return jnp.concatenate(tiles, axis=0)


def masked(block, gen, rank):
    rows = lax.broadcasted_iota(jnp.int32, (N, N), 0)
    cols = lax.broadcasted_iota(jnp.int32, (N, N), 1)
    identity = jnp.where(rows == cols, 1.0, 0.0)
    block = jnp.where((rows < rank) & (cols < rank), block, identity)
    inside = lax.broadcasted_iota(jnp.int32, (N, K), 0) < rank
    return block, jnp.where(inside, gen, 0.0)


def merge_kernel(height, place, ranks, gathered, mixing_own, mixing_near, mixing_far, *refs):
    last = height == LEVELS - 1
    leaf, member = place[0], place[1]
    base = leaf >> height + 1 << height + 1
    low_rank = ranks[base + 2**height - 1]
    high_rank = ranks[base + 2 ** (height + 1) - 1]
    upper = leaf >> height & 1 == 1
    held = 8 if last else 6
    refs, scratch = refs[:-held], refs[-held:]
    peer_block, peer_gen = unpack(gathered)
    if height == 0:
        own_block, own_gen = unpack(refs[0])
        outs = refs[1:]
        mixing = unpack_first(upper, member & 1, mixing_own, mixing_near, mixing_far)
    else:
        own_block, own_gen = refs[0][...], refs[1][...]
        outs = refs[2:]
        mixing = unpack_mixing(height, member >> 1 & 1, member & 1, mixing_own, mixing_near, mixing_far)
    low_block = jnp.where(upper, peer_block, own_block)
    high_block = jnp.where(upper, own_block, peer_block)
    low_gen = jnp.where(upper, peer_gen, own_gen)
    high_gen = jnp.where(upper, own_gen, peer_gen)
    if height == 0:
        low_block, low_gen = masked(low_block, low_gen, low_rank)
        high_block, high_gen = masked(high_block, high_gen, high_rank)
    rows = lax.broadcasted_iota(jnp.int32, (N, N), 0)
    cols = lax.broadcasted_iota(jnp.int32, (N, N), 1)
    inside = (rows < high_rank) & (cols < low_rank)
    solved_ref, inverse_ref, above_ref, mixing_ref, block_ref, gen_ref = outs[:6]
    low_ref, high_ref, low_gen_ref, high_gen_ref, mixed_ref, rest_ref = scratch[:6]
    if last:
        block_ref, gen_ref = scratch[6:]
    mixing_ref[...] = jnp.where(inside, mixing, 0.0)
    low_ref[...], high_ref[...] = low_block, high_block
    low_gen_ref[...], high_gen_ref[...] = low_gen, high_gen

    def part(i):
        return pl.ds(pl.multiple_of(i * T, T), T)

    @pl.loop(0, N // T)
    def _(i):
        at = part(i)
        mixed_ref[at, :] = dot(high_ref[at, :], mixing_ref[...])
        rest_ref[at, 2 * N :] = low_gen_ref[at, :] + dot(mixing_ref[:, at], high_gen_ref[...], 0, 0)

    @pl.loop(0, N // T)
    def _(i):
        at = part(i)
        gen_input = rest_ref[at, 2 * N :]
        products = dot(gen_input, jnp.concatenate([rest_ref[:, 2 * N :], high_gen_ref[...]], axis=0), 1, 1)
        rest_ref[at, :N] = low_ref[at, :] + products[:, :N] + dot(mixing_ref[:, at], mixed_ref[...], 0, 0)
        rest_ref[at, N : 2 * N] = products[:, N:] + mixed_ref[:, at].T

    @pl.loop(0, N // T)
    def _(i):
        at = part(i)
        inverse = inverse_factor(rest_ref[at, at])
        inverse_ref[i] = inverse
        for step in range(N // T):

            @pl.when(i == step)
            def _():
                top, low = T * step, T * (step + 1)
                done = dot(inverse, rest_ref[top:low, low:])
                rest_ref[top:low, low:] = done
                if low < N:
                    rest_ref[low:, low:] -= dot(done[:, : N - low], done, 0, 0)

    solved_ref[...] = rest_ref[:, N : 2 * N]
    above_ref[...] = rest_ref[:, :N]

    @pl.loop(0, N // T)
    def _(i):
        at = part(i)
        products = dot(solved_ref[:, at], rest_ref[:, N:], 0, 0)
        block_ref[at, :] = high_ref[at, :] + dot(high_gen_ref[at, :], high_gen_ref[...], 1, 1) - products[:, :N]
        gen_ref[at, :] = high_gen_ref[at, :] - products[:, N:]

    own = pl.ds(pl.multiple_of(member * SHARE, 8), SHARE)
    if last:
        outs[4][...] = block_ref[own, :]
        outs[5][...] = gen_ref[own, :]
    else:
        share_ref = outs[6]
        share_ref[:SHARE, :] = block_ref[own, :]
        third = SHARE // 3
        for q in range(3):
            at = pl.ds(pl.multiple_of(member * SHARE + q * third, 8), third)
            share_ref[SHARE:, K * q : K * (q + 1)] = gen_ref[at, :]


def merge(height, place, ranks, gathered, mixing, own):
    last = height == LEVELS - 1
    shapes = [(N, N), (N // T, T, T), (N, N), (N, N)]
    shapes += [(SHARE, N), (SHARE, K)] if last else [(N, N), (N, K), (PACK, N)]
    kept = [(N, N), (N, N), (N, K), (N, K), (N, N), (N, 2 * N + K)] + ([(N, N), (N, K)] if last else [])
    return pl.pallas_call(
        functools.partial(merge_kernel, height),
        out_shape=[jax.ShapeDtypeStruct(shape, jnp.float32) for shape in shapes],
        in_specs=[SMEM, SMEM] + [VMEM] * (4 + len(own)),
        out_specs=[VMEM] * len(shapes),
        scratch_shapes=[pltpu.VMEM(shape, jnp.float32) for shape in kept],
        compiler_params=pltpu.CompilerParams(vmem_limit_bytes=40 * 2**20),
        cost_estimate=pl.CostEstimate(flops=2 * 10**10, transcendentals=0, bytes_accessed=8 * 10**6),
        name="merge%d" % height,
    )(place, ranks, gathered, *mixing, *own)


def rhs_kernel(height, place, ranks, solved, inverses, above, mixing, own, peer, out):
    leaf = place[0]
    upper = leaf >> height & 1 == 1
    low = jnp.where(upper, peer[...], own[...])
    high = jnp.where(upper, own[...], peer[...])
    if height == 0:
        base = leaf >> 1 << 1
        rows = lax.broadcasted_iota(jnp.int32, low.shape, 0)
        low = jnp.where(rows < ranks[base], low, 0.0)
        high = jnp.where(rows < ranks[base + 1], high, 0.0)
    rest = low + dot(mixing[...], high, 0, 0)
    done = []
    for i in range(N // T):
        done.append(dot(inverses[i], rest[:T]))
        at = T * (i + 1)
        if at < N:
            rest = rest[T:] - dot(above[T * i : at, at:], done[-1], 0, 0)
    out[...] = high - dot(solved[...], jnp.concatenate(done, axis=0), 0, 0)


def merge_rhs(height, place, ranks, solved, inverses, above, mixing, own, peer):
    return pl.pallas_call(
        functools.partial(rhs_kernel, height),
        out_shape=jax.ShapeDtypeStruct(own.shape, jnp.float32),
        in_specs=[SMEM, SMEM] + [VMEM] * 6,
        out_specs=VMEM,
        compiler_params=pltpu.CompilerParams(vmem_limit_bytes=24 * 2**20),
        cost_estimate=pl.CostEstimate(flops=3 * 10**9, transcendentals=0, bytes_accessed=3 * 10**6),
        name="rhs%d" % height,
    )(place, ranks, solved, inverses, above, mixing, own, peer)


def swapped(block, bit):
    route = []
    for low in range(16):
        if bit < 3:
            high = low ^ 1 << bit
        else:
            high = (low + 4 if low >> 2 & 1 else low - 4) % 16
        route.append((low, high))
    return lax.ppermute(block, Z, route)


def joined(own, peer, bit):
    upper = lax.axis_index("z%d" % bit) == 1
    return jnp.where(upper, jnp.concatenate([peer, own]), jnp.concatenate([own, peer]))


def across_core(block):
    return lax.ppermute(block, "c", [(0, 1), (1, 0)])


def across_chip(block):
    return lax.ppermute(block, "y", [(0, 1), (1, 0), (2, 3), (3, 2)])


def spread(share):
    return lax.all_gather(share, GRP, axis=0)


def on_device(diag_block, generator, right_sides, *rest):
    pieces, node_ranks = rest[:LEVELS], rest[LEVELS]
    leaf = lax.axis_index(LEAF)
    member = lax.axis_index(GRP)
    core = lax.axis_index("c")
    quarter = 2 * (lax.axis_index("y") & 1) + core
    place = jnp.where(jnp.arange(2) == 0, leaf, member).astype(jnp.int32)
    third = SHARE // 3
    packed_gen = jnp.concatenate([generator[third * q : third * (q + 1)] for q in range(3)], axis=1)
    share = jnp.concatenate([diag_block, packed_gen], axis=0)
    tiles = []
    for height, piece in enumerate(pieces):
        count = piece.shape[0] // MIXED[height]
        at = (quarter if height else core) % count * MIXED[height]
        tiles.append(lax.dynamic_slice_in_dim(piece, at, MIXED[height], 0))

    def step(bit, start):
        moved = tiles[start:]
        return swapped(jnp.concatenate(moved, axis=0), bit)

    def join(received, bit, start):
        offset = 0
        for height in range(start, LEVELS):
            count = tiles[height].shape[0]
            tiles[height] = joined(tiles[height], received[offset : offset + count], bit)
            offset += count

    peer_share = swapped(share, 0)
    near = swapped(tiles[0], 0)
    moving = step(0, 1)
    own_all = spread(share)
    peer_share, near, moving, own_all = lax.optimization_barrier((peer_share, near, moving, own_all))
    mixing = (pieces[0], near, across_core(near))
    join(moving, 0, 1)
    moving = step(1, 1)
    rhs_now = right_sides
    peer_rhs = swapped(rhs_now, 0)
    gathered = spread(peer_share)
    own = (own_all,)
    for height in range(LEVELS):
        made = merge(height, place, node_ranks, gathered, mixing, own)
        factors, own = made[:4], made[4:6]
        if height == LEVELS - 1:
            rhs_now = merge_rhs(height, place, node_ranks, *factors, rhs_now, peer_rhs)
            break
        if height + 1 < LEVELS and moving is not None:
            share, peer_rhs, moving = lax.optimization_barrier((made[6], peer_rhs, moving))
        else:
            share, peer_rhs = lax.optimization_barrier((made[6], peer_rhs))
        peer_share = swapped(share, height + 1)
        if moving is not None:
            join(moving, height + 1, height + 1)
        tile = tiles[height + 1]
        near = across_chip(tile)
        mixing = (tile, near, across_core(jnp.concatenate([tile, near], axis=0)))
        rhs_now = merge_rhs(height, place, node_ranks, *factors, rhs_now, peer_rhs)
        peer_share, rhs_now = lax.optimization_barrier((peer_share, rhs_now))
        peer_rhs = swapped(rhs_now, height + 1)
        gathered = spread(peer_share)
        moving = None
        if height + 2 < LEVELS:
            gathered, *tiles[height + 2 :] = lax.optimization_barrier((gathered, *tiles[height + 2 :]))
            moving = step(height + 2, height + 2)
    return (own[0], own[1], rhs_now)


def solution(mesh):
    fine = Mesh(mesh.devices.reshape(4, 2, 2, 2, 2, 4, 2), LEAF + GRP)
    rows = P(LEAF + GRP, None)
    leaves = P(LEAF, None)
    columns = P(LEAF, GRP)
    return jax.shard_map(
        on_device,
        mesh=fine,
        in_specs=(rows, rows, columns, leaves, leaves, leaves, leaves, P()),
        out_specs=(rows, rows, columns),
        check_vma=False,
    )
```

```python
import functools

import jax
import jax.numpy as jnp
from jax import lax
from jax.experimental import pallas as pl
from jax.experimental.pallas import tpu as pltpu
from jax.sharding import Mesh, PartitionSpec as P

LEVELS = 4
N = 384
K = 128
T = 128
W = 16
SHARE = 48
PACK = 64
LOWER = ((0, 0), (1, 0), (1, 1), (2, 0), (2, 1), (2, 2))
QUARTER = (6 * T + N) // 4
LEAF = ("x", "z3", "z2", "z1", "z0")
GRP = ("y", "c")
Z = ("z3", "z2", "z1", "z0")
MIXED = (96, 24, 16, 8)
HIGHEST = lax.Precision.HIGHEST
VMEM = pl.BlockSpec(memory_space=pltpu.VMEM)
SMEM = pl.BlockSpec(memory_space=pltpu.SMEM)


def dot(first, second, first_axis=1, second_axis=0):
    return lax.dot_general(
        first,
        second,
        (((first_axis,), (second_axis,)), ((), ())),
        precision=HIGHEST,
        preferred_element_type=jnp.float32,
    )


def wide(values):
    return jnp.broadcast_to(values, (8, T))


def sweep_panel(rows, start):
    lanes = lax.broadcasted_iota(jnp.int32, (8, T), 1)
    subs = lax.broadcasted_iota(jnp.int32, (8, T), 0)
    cols = [[wide(part[:, start + m : start + m + 1]) for part in rows] for m in range(W)]
    factor = [jnp.zeros((8, T), jnp.float32) for _ in rows]
    for k in range(W):
        group, sub = divmod(k, 8)
        here = subs == sub
        pivot = wide(cols[k][group][sub : sub + 1, :])
        inverse = 1.0 / pivot
        mult = list(cols[k])
        mult[group] = jnp.where(here, -1.0, mult[group])
        for m in range(k + 1, W):
            step = wide(cols[m][group][sub : sub + 1, :]) * inverse
            kept = list(cols[m])
            kept[group] = jnp.where(here, 0.0, kept[group])
            cols[m] = [part - q * step for part, q in zip(kept, mult)]
        lane = lanes == start + k
        row = jnp.where(lane, 1.0, wide(rows[group][sub : sub + 1, :]))
        scaled = jnp.where(lanes <= start + k, row, 0.0) * lax.rsqrt(pivot)
        factor[group] = jnp.where(here, scaled, factor[group])
        step = row * inverse
        kept = [jnp.where(lane | here if i == group else lane, 0.0, part) for i, part in enumerate(rows)]
        rows = [part - q * step for part, q in zip(kept, mult)]
    return rows, factor


def inverse_factor(block):
    lanes = lax.broadcasted_iota(jnp.int32, (8, T), 1)
    rows = [block[8 * i : 8 * i + 8, :] for i in range(W // 8)]
    below = block[W:]
    out = []
    for start in range(0, T, W):
        swept, factor = sweep_panel(rows, start)
        out += factor
        if start + W == T:
            break
        panel = jnp.concatenate(swept, axis=0)
        inside = (lanes >= start) & (lanes < start + W)
        rows = []
        for i in range(W // 8):
            part = below[8 * i : 8 * i + 8, :]
            total = jnp.where(inside, 0.0, part)
            for k in range(W):
                total = total - wide(part[:, start + k : start + k + 1]) * wide(panel[k : k + 1, :])
            rows.append(total)
        if start + 2 * W < T:
            below = below[W:]
            drop = dot(below[:, start : start + W], panel)
            span = lax.broadcasted_iota(jnp.int32, below.shape, 1)
            below = jnp.where((span >= start) & (span < start + W), 0.0, below) - drop
    return jnp.concatenate(out, axis=0)


def unpack(gathered):
    block = jnp.concatenate([gathered[g, :SHARE, :] for g in range(8)], axis=0)
    gen = jnp.concatenate(
        [gathered[g, SHARE:PACK, K * q : K * (q + 1)] for g in range(8) for q in range(3)], axis=0
    )
    return block, gen


def unpack_quarters(gathered, row, packed):
    for r in range(2):
        for c in range(2):
            at = QUARTER * (2 * r + c)
            packed[at : at + QUARTER, :] = gathered[c, row ^ r]
    tiles = {}
    for k, (i, j) in enumerate(LOWER):
        tiles[i, j] = packed[T * k : T * (k + 1), :]
        tiles[j, i] = tiles[i, j] if i == j else tiles[i, j].T
    block = jnp.concatenate(
        [jnp.concatenate([tiles[i, j] for j in range(3)], axis=1) for i in range(3)], axis=0
    )
    return block, packed[T * len(LOWER) :, :]


def unpack_first(upper, core, own, near, far):
    even = core == 0
    peer = [jnp.where(even, near[...], far[...]), jnp.where(even, far[...], near[...])]
    peer = jnp.concatenate(peer, axis=0)
    return jnp.concatenate([jnp.where(upper, peer, own[...]), jnp.where(upper, own[...], peer)], axis=0)


def unpack_mixing(height, row, core, own, near, far):
    count = own.shape[0]
    front, even = row == 0, core == 0
    own, near, close, apart = own[...], near[...], far[:count, :], far[count:, :]
    mine = [jnp.where(front, own, near), jnp.where(front, near, own)]
    theirs = [jnp.where(front, close, apart), jnp.where(front, apart, close)]
    parts = []
    for first, second in zip(mine, theirs):
        parts += [jnp.where(even, first, second), jnp.where(even, second, first)]
    rows = MIXED[height]
    tiles = []
    for sub in range(2 << height):
        for part in range((N >> height + 1) // rows):
            tiles.append(parts[part][sub * rows : (sub + 1) * rows, :])
    return jnp.concatenate(tiles, axis=0)


def masked(block, gen, rank):
    rows = lax.broadcasted_iota(jnp.int32, (N, N), 0)
    cols = lax.broadcasted_iota(jnp.int32, (N, N), 1)
    identity = jnp.where(rows == cols, 1.0, 0.0)
    block = jnp.where((rows < rank) & (cols < rank), block, identity)
    inside = lax.broadcasted_iota(jnp.int32, (N, K), 0) < rank
    return block, jnp.where(inside, gen, 0.0)


def merge_kernel(height, place, ranks, gathered, mixing_own, mixing_near, mixing_far, *refs):
    last = height == LEVELS - 1
    leaf, member = place[0], place[1]
    base = leaf >> height + 1 << height + 1
    low_rank = ranks[base + 2**height - 1]
    high_rank = ranks[base + 2 ** (height + 1) - 1]
    upper = leaf >> height & 1 == 1
    held = 9 if last else 7
    refs, scratch = refs[:-held], refs[-held:]
    packed_ref = scratch[6]
    row = member >> 1 & 1
    if height == 0:
        peer_block, peer_gen = unpack(gathered)
        own_block, own_gen = unpack(refs[0])
        outs = refs[1:]
        mixing = unpack_first(upper, member & 1, mixing_own, mixing_near, mixing_far)
    else:
        peer_block, peer_gen = unpack_quarters(gathered, row, packed_ref)
        own_block, own_gen = refs[0][...], refs[1][...]
        outs = refs[2:]
        mixing = unpack_mixing(height, row, member & 1, mixing_own, mixing_near, mixing_far)
    low_block = jnp.where(upper, peer_block, own_block)
    high_block = jnp.where(upper, own_block, peer_block)
    low_gen = jnp.where(upper, peer_gen, own_gen)
    high_gen = jnp.where(upper, own_gen, peer_gen)
    if height == 0:
        low_block, low_gen = masked(low_block, low_gen, low_rank)
        high_block, high_gen = masked(high_block, high_gen, high_rank)
    rows = lax.broadcasted_iota(jnp.int32, (N, N), 0)
    cols = lax.broadcasted_iota(jnp.int32, (N, N), 1)
    inside = (rows < high_rank) & (cols < low_rank)
    solved_ref, inverse_ref, above_ref, mixing_ref, block_ref, gen_ref = outs[:6]
    low_ref, high_ref, low_gen_ref, high_gen_ref, mixed_ref, rest_ref = scratch[:6]
    if last:
        block_ref, gen_ref = scratch[7:]
    mixing_ref[...] = jnp.where(inside, mixing, 0.0)
    low_ref[...], high_ref[...] = low_block, high_block
    low_gen_ref[...], high_gen_ref[...] = low_gen, high_gen

    def part(i):
        return pl.ds(pl.multiple_of(i * T, T), T)

    @pl.loop(0, N // T)
    def _(i):
        at = part(i)
        mixed_ref[at, :] = dot(high_ref[at, :], mixing_ref[...])
        rest_ref[at, 2 * N :] = low_gen_ref[at, :] + dot(mixing_ref[:, at], high_gen_ref[...], 0, 0)

    @pl.loop(0, N // T)
    def _(i):
        at = part(i)
        gen_input = rest_ref[at, 2 * N :]
        products = dot(gen_input, jnp.concatenate([rest_ref[:, 2 * N :], high_gen_ref[...]], axis=0), 1, 1)
        rest_ref[at, :N] = low_ref[at, :] + products[:, :N] + dot(mixing_ref[:, at], mixed_ref[...], 0, 0)
        rest_ref[at, N : 2 * N] = products[:, N:] + mixed_ref[:, at].T

    @pl.loop(0, N // T)
    def _(i):
        at = part(i)
        inverse = inverse_factor(rest_ref[at, at])
        inverse_ref[i] = inverse
        for step in range(N // T):

            @pl.when(i == step)
            def _():
                top, low = T * step, T * (step + 1)
                done = dot(inverse, rest_ref[top:low, low:])
                rest_ref[top:low, low:] = done
                if low < N:
                    rest_ref[low:, low:] -= dot(done[:, : N - low], done, 0, 0)

    solved_ref[...] = rest_ref[:, N : 2 * N]
    above_ref[...] = rest_ref[:, :N]

    @pl.loop(0, N // T)
    def _(i):
        at = part(i)
        products = dot(solved_ref[:, at], rest_ref[:, N:], 0, 0)
        block_ref[at, :] = high_ref[at, :] + dot(high_gen_ref[at, :], high_gen_ref[...], 1, 1) - products[:, :N]
        gen_ref[at, :] = high_gen_ref[at, :] - products[:, N:]

    own = pl.ds(pl.multiple_of(member * SHARE, 8), SHARE)
    if last:
        outs[4][...] = block_ref[own, :]
        outs[5][...] = gen_ref[own, :]
    else:
        for k, (i, j) in enumerate(LOWER):
            packed_ref[T * k : T * (k + 1), :] = block_ref[T * i : T * (i + 1), T * j : T * (j + 1)]
        packed_ref[T * len(LOWER) :, :] = gen_ref[...]
        quarter = 2 * row + (member & 1)
        outs[6][...] = packed_ref[pl.ds(pl.multiple_of(quarter * QUARTER, 8), QUARTER), :]


def merge(height, place, ranks, gathered, mixing, own):
    last = height == LEVELS - 1
    shapes = [(N, N), (N // T, T, T), (N, N), (N, N)]
    shapes += [(SHARE, N), (SHARE, K)] if last else [(N, N), (N, K), (QUARTER, T)]
    kept = [(N, N), (N, N), (N, K), (N, K), (N, N), (N, 2 * N + K), (4 * QUARTER, T)] + ([(N, N), (N, K)] if last else [])
    return pl.pallas_call(
        functools.partial(merge_kernel, height),
        out_shape=[jax.ShapeDtypeStruct(shape, jnp.float32) for shape in shapes],
        in_specs=[SMEM, SMEM] + [VMEM] * (4 + len(own)),
        out_specs=[VMEM] * len(shapes),
        scratch_shapes=[pltpu.VMEM(shape, jnp.float32) for shape in kept],
        compiler_params=pltpu.CompilerParams(vmem_limit_bytes=40 * 2**20),
        cost_estimate=pl.CostEstimate(flops=2 * 10**10, transcendentals=0, bytes_accessed=8 * 10**6),
        name="merge%d" % height,
    )(place, ranks, gathered, *mixing, *own)


def rhs_kernel(height, place, ranks, solved, inverses, above, mixing, own, peer, out):
    leaf = place[0]
    upper = leaf >> height & 1 == 1
    low = jnp.where(upper, peer[...], own[...])
    high = jnp.where(upper, own[...], peer[...])
    if height == 0:
        base = leaf >> 1 << 1
        rows = lax.broadcasted_iota(jnp.int32, low.shape, 0)
        low = jnp.where(rows < ranks[base], low, 0.0)
        high = jnp.where(rows < ranks[base + 1], high, 0.0)
    rest = low + dot(mixing[...], high, 0, 0)
    done = []
    for i in range(N // T):
        done.append(dot(inverses[i], rest[:T]))
        at = T * (i + 1)
        if at < N:
            rest = rest[T:] - dot(above[T * i : at, at:], done[-1], 0, 0)
    out[...] = high - dot(solved[...], jnp.concatenate(done, axis=0), 0, 0)


def merge_rhs(height, place, ranks, solved, inverses, above, mixing, own, peer):
    return pl.pallas_call(
        functools.partial(rhs_kernel, height),
        out_shape=jax.ShapeDtypeStruct(own.shape, jnp.float32),
        in_specs=[SMEM, SMEM] + [VMEM] * 6,
        out_specs=VMEM,
        compiler_params=pltpu.CompilerParams(vmem_limit_bytes=24 * 2**20),
        cost_estimate=pl.CostEstimate(flops=3 * 10**9, transcendentals=0, bytes_accessed=3 * 10**6),
        name="rhs%d" % height,
    )(place, ranks, solved, inverses, above, mixing, own, peer)


def swapped(block, bit):
    route = []
    for low in range(16):
        if bit < 3:
            high = low ^ 1 << bit
        else:
            high = (low + 4 if low >> 2 & 1 else low - 4) % 16
        route.append((low, high))
    return lax.ppermute(block, Z, route)


def joined(own, peer, bit):
    upper = lax.axis_index("z%d" % bit) == 1
    return jnp.where(upper, jnp.concatenate([peer, own]), jnp.concatenate([own, peer]))


def across_core(block):
    return lax.ppermute(block, "c", [(0, 1), (1, 0)])


def across_chip(block):
    return lax.ppermute(block, "y", [(0, 1), (1, 0), (2, 3), (3, 2)])


def spread(share):
    return lax.all_gather(share, GRP, axis=0)


def on_device(diag_block, generator, right_sides, *rest):
    pieces, node_ranks = rest[:LEVELS], rest[LEVELS]
    leaf = lax.axis_index(LEAF)
    member = lax.axis_index(GRP)
    core = lax.axis_index("c")
    quarter = 2 * (lax.axis_index("y") & 1) + core
    place = jnp.where(jnp.arange(2) == 0, leaf, member).astype(jnp.int32)
    third = SHARE // 3
    packed_gen = jnp.concatenate([generator[third * q : third * (q + 1)] for q in range(3)], axis=1)
    share = jnp.concatenate([diag_block, packed_gen], axis=0)
    tiles = []
    for height, piece in enumerate(pieces):
        count = piece.shape[0] // MIXED[height]
        at = (quarter if height else core) % count * MIXED[height]
        tiles.append(lax.dynamic_slice_in_dim(piece, at, MIXED[height], 0))

    def step(bit, start):
        moved = tiles[start:]
        return swapped(jnp.concatenate(moved, axis=0), bit)

    def join(received, bit, start):
        offset = 0
        for height in range(start, LEVELS):
            count = tiles[height].shape[0]
            tiles[height] = joined(tiles[height], received[offset : offset + count], bit)
            offset += count

    peer_share = swapped(share, 0)
    near = swapped(tiles[0], 0)
    moving = step(0, 1)
    own_all = spread(share)
    peer_share, near, moving, own_all = lax.optimization_barrier((peer_share, near, moving, own_all))
    mixing = (pieces[0], near, across_core(near))
    join(moving, 0, 1)
    moving = step(1, 1)
    rhs_now = right_sides
    peer_rhs = swapped(rhs_now, 0)
    gathered = spread(peer_share)
    own = (own_all,)
    for height in range(LEVELS):
        made = merge(height, place, node_ranks, gathered, mixing, own)
        factors, own = made[:4], made[4:6]
        if height == LEVELS - 1:
            rhs_now = merge_rhs(height, place, node_ranks, *factors, rhs_now, peer_rhs)
            break
        if height + 1 < LEVELS and moving is not None:
            share, peer_rhs, moving = lax.optimization_barrier((made[6], peer_rhs, moving))
        else:
            share, peer_rhs = lax.optimization_barrier((made[6], peer_rhs))
        peer_share = swapped(share, height + 1)
        if moving is not None:
            join(moving, height + 1, height + 1)
        tile = tiles[height + 1]
        near = across_chip(tile)
        mixing = (tile, near, across_core(jnp.concatenate([tile, near], axis=0)))
        rhs_now = merge_rhs(height, place, node_ranks, *factors, rhs_now, peer_rhs)
        peer_share, rhs_now = lax.optimization_barrier((peer_share, rhs_now))
        peer_rhs = swapped(rhs_now, height + 1)
        halves = jnp.stack([peer_share, across_chip(peer_share)])
        gathered = lax.all_gather(halves, "c", axis=0)
        moving = None
        if height + 2 < LEVELS:
            gathered, *tiles[height + 2 :] = lax.optimization_barrier((gathered, *tiles[height + 2 :]))
            moving = step(height + 2, height + 2)
    return (own[0], own[1], rhs_now)


def solution(mesh):
    fine = Mesh(mesh.devices.reshape(4, 2, 2, 2, 2, 4, 2), LEAF + GRP)
    rows = P(LEAF + GRP, None)
    leaves = P(LEAF, None)
    columns = P(LEAF, GRP)
    return jax.shard_map(
        on_device,
        mesh=fine,
        in_specs=(rows, rows, columns, leaves, leaves, leaves, leaves, P()),
        out_specs=(rows, rows, columns),
        check_vma=False,
    )
```

```python
import functools

import jax
import jax.numpy as jnp
from jax import lax
from jax.experimental import pallas as pl
from jax.experimental.pallas import tpu as pltpu
from jax.sharding import Mesh, PartitionSpec as P

LEVELS = 4
N = 384
K = 128
T = 128
W = 16
SHARE = 48
PACK = 64
LOWER = ((0, 0), (1, 0), (1, 1), (2, 0), (2, 1), (2, 2))
QUARTER = (6 * T + N) // 4
LEAF = ("x", "z3", "z2", "z1", "z0")
GRP = ("y", "c")
Z = ("z3", "z2", "z1", "z0")
MIXED = (96, 24, 16, 8)
HIGHEST = lax.Precision.HIGHEST
VMEM = pl.BlockSpec(memory_space=pltpu.VMEM)
SMEM = pl.BlockSpec(memory_space=pltpu.SMEM)


def dot(first, second, first_axis=1, second_axis=0):
    return lax.dot_general(
        first,
        second,
        (((first_axis,), (second_axis,)), ((), ())),
        precision=HIGHEST,
        preferred_element_type=jnp.float32,
    )


def wide(values):
    return jnp.broadcast_to(values, (8, T))


def sweep_panel(rows, start):
    lanes = lax.broadcasted_iota(jnp.int32, (8, T), 1)
    subs = lax.broadcasted_iota(jnp.int32, (8, T), 0)
    cols = [[wide(part[:, start + m : start + m + 1]) for part in rows] for m in range(W)]
    factor = [jnp.zeros((8, T), jnp.float32) for _ in rows]
    for k in range(W):
        group, sub = divmod(k, 8)
        here = subs == sub
        pivot = wide(cols[k][group][sub : sub + 1, :])
        inverse = 1.0 / pivot
        mult = list(cols[k])
        mult[group] = jnp.where(here, -1.0, mult[group])
        for m in range(k + 1, W):
            step = wide(cols[m][group][sub : sub + 1, :]) * inverse
            kept = list(cols[m])
            kept[group] = jnp.where(here, 0.0, kept[group])
            cols[m] = [part - q * step for part, q in zip(kept, mult)]
        lane = lanes == start + k
        row = jnp.where(lane, 1.0, wide(rows[group][sub : sub + 1, :]))
        scaled = jnp.where(lanes <= start + k, row, 0.0) * lax.rsqrt(pivot)
        factor[group] = jnp.where(here, scaled, factor[group])
        step = row * inverse
        kept = [jnp.where(lane | here if i == group else lane, 0.0, part) for i, part in enumerate(rows)]
        rows = [part - q * step for part, q in zip(kept, mult)]
    return rows, factor


def inverse_factor(block):
    lanes = lax.broadcasted_iota(jnp.int32, (8, T), 1)
    rows = [block[8 * i : 8 * i + 8, :] for i in range(W // 8)]
    below = block[W:]
    out = []
    for start in range(0, T, W):
        swept, factor = sweep_panel(rows, start)
        out += factor
        if start + W == T:
            break
        panel = jnp.concatenate(swept, axis=0)
        inside = (lanes >= start) & (lanes < start + W)
        rows = []
        for i in range(W // 8):
            part = below[8 * i : 8 * i + 8, :]
            total = jnp.where(inside, 0.0, part)
            for k in range(W):
                total = total - wide(part[:, start + k : start + k + 1]) * wide(panel[k : k + 1, :])
            rows.append(total)
        if start + 2 * W < T:
            below = below[W:]
            drop = dot(below[:, start : start + W], panel)
            span = lax.broadcasted_iota(jnp.int32, below.shape, 1)
            below = jnp.where((span >= start) & (span < start + W), 0.0, below) - drop
    return jnp.concatenate(out, axis=0)


def unpack(mine, theirs, member, first):
    blocks, gens = [], []
    for y in range(4):
        away = (member >> 1) - y & 3
        here, there = mine[away, first : first + PACK, :], theirs[away, first : first + PACK, :]
        even = member & 1 == 0
        for share in (jnp.where(even, here, there), jnp.where(even, there, here)):
            blocks.append(share[:SHARE])
            gens += [share[SHARE:, K * q : K * (q + 1)] for q in range(3)]
    return jnp.concatenate(blocks, axis=0), jnp.concatenate(gens, axis=0)


def unpack_quarters(gathered, row, packed):
    for r in range(2):
        for c in range(2):
            at = QUARTER * (2 * r + c)
            packed[at : at + QUARTER, :] = gathered[c, row ^ r]
    tiles = {}
    for k, (i, j) in enumerate(LOWER):
        tiles[i, j] = packed[T * k : T * (k + 1), :]
        tiles[j, i] = tiles[i, j] if i == j else tiles[i, j].T
    block = jnp.concatenate(
        [jnp.concatenate([tiles[i, j] for j in range(3)], axis=1) for i in range(3)], axis=0
    )
    return block, packed[T * len(LOWER) :, :]


def unpack_first(upper, core, own, near, far):
    even = core == 0
    peer = [jnp.where(even, near[...], far[...]), jnp.where(even, far[...], near[...])]
    peer = jnp.concatenate(peer, axis=0)
    return jnp.concatenate([jnp.where(upper, peer, own[...]), jnp.where(upper, own[...], peer)], axis=0)


def unpack_mixing(height, row, core, own, near, far):
    count = own.shape[0]
    front, even = row == 0, core == 0
    own, near, close, apart = own[...], near[...], far[:count, :], far[count:, :]
    mine = [jnp.where(front, own, near), jnp.where(front, near, own)]
    theirs = [jnp.where(front, close, apart), jnp.where(front, apart, close)]
    parts = []
    for first, second in zip(mine, theirs):
        parts += [jnp.where(even, first, second), jnp.where(even, second, first)]
    rows = MIXED[height]
    tiles = []
    for sub in range(2 << height):
        for part in range((N >> height + 1) // rows):
            tiles.append(parts[part][sub * rows : (sub + 1) * rows, :])
    return jnp.concatenate(tiles, axis=0)


def masked(block, gen, rank):
    rows = lax.broadcasted_iota(jnp.int32, (N, N), 0)
    cols = lax.broadcasted_iota(jnp.int32, (N, N), 1)
    identity = jnp.where(rows == cols, 1.0, 0.0)
    block = jnp.where((rows < rank) & (cols < rank), block, identity)
    inside = lax.broadcasted_iota(jnp.int32, (N, K), 0) < rank
    return block, jnp.where(inside, gen, 0.0)


def merge_kernel(height, place, ranks, gathered, mixing_own, mixing_near, mixing_far, *refs):
    last = height == LEVELS - 1
    leaf, member = place[0], place[1]
    base = leaf >> height + 1 << height + 1
    low_rank = ranks[base + 2**height - 1]
    high_rank = ranks[base + 2 ** (height + 1) - 1]
    upper = leaf >> height & 1 == 1
    held = 9 if last else 7
    refs, scratch = refs[:-held], refs[-held:]
    packed_ref = scratch[6]
    row = member >> 1 & 1
    if height == 0:
        own_block, own_gen = unpack(gathered, refs[0], member, 0)
        peer_block, peer_gen = unpack(gathered, refs[0], member, PACK)
        outs = refs[1:]
        mixing = unpack_first(upper, member & 1, mixing_own, mixing_near, mixing_far)
    else:
        peer_block, peer_gen = unpack_quarters(gathered, row, packed_ref)
        own_block, own_gen = refs[0][...], refs[1][...]
        outs = refs[2:]
        mixing = unpack_mixing(height, row, member & 1, mixing_own, mixing_near, mixing_far)
    low_block = jnp.where(upper, peer_block, own_block)
    high_block = jnp.where(upper, own_block, peer_block)
    low_gen = jnp.where(upper, peer_gen, own_gen)
    high_gen = jnp.where(upper, own_gen, peer_gen)
    if height == 0:
        low_block, low_gen = masked(low_block, low_gen, low_rank)
        high_block, high_gen = masked(high_block, high_gen, high_rank)
    rows = lax.broadcasted_iota(jnp.int32, (N, N), 0)
    cols = lax.broadcasted_iota(jnp.int32, (N, N), 1)
    inside = (rows < high_rank) & (cols < low_rank)
    solved_ref, inverse_ref, above_ref, mixing_ref, block_ref, gen_ref = outs[:6]
    low_ref, high_ref, low_gen_ref, high_gen_ref, mixed_ref, rest_ref = scratch[:6]
    if last:
        block_ref, gen_ref = scratch[7:]
    mixing_ref[...] = jnp.where(inside, mixing, 0.0)
    low_ref[...], high_ref[...] = low_block, high_block
    low_gen_ref[...], high_gen_ref[...] = low_gen, high_gen

    def part(i):
        return pl.ds(pl.multiple_of(i * T, T), T)

    @pl.loop(0, N // T)
    def _(i):
        at = part(i)
        mixed_ref[at, :] = dot(high_ref[at, :], mixing_ref[...])
        rest_ref[at, 2 * N :] = low_gen_ref[at, :] + dot(mixing_ref[:, at], high_gen_ref[...], 0, 0)

    @pl.loop(0, N // T)
    def _(i):
        at = part(i)
        gen_input = rest_ref[at, 2 * N :]
        products = dot(gen_input, jnp.concatenate([rest_ref[:, 2 * N :], high_gen_ref[...]], axis=0), 1, 1)
        rest_ref[at, :N] = low_ref[at, :] + products[:, :N] + dot(mixing_ref[:, at], mixed_ref[...], 0, 0)
        rest_ref[at, N : 2 * N] = products[:, N:] + mixed_ref[:, at].T

    @pl.loop(0, N // T)
    def _(i):
        at = part(i)
        inverse = inverse_factor(rest_ref[at, at])
        inverse_ref[i] = inverse
        for step in range(N // T):

            @pl.when(i == step)
            def _():
                top, low = T * step, T * (step + 1)
                done = dot(inverse, rest_ref[top:low, low:])
                rest_ref[top:low, low:] = done
                if low < N:
                    rest_ref[low:, low:] -= dot(done[:, : N - low], done, 0, 0)

    solved_ref[...] = rest_ref[:, N : 2 * N]
    above_ref[...] = rest_ref[:, :N]

    @pl.loop(0, N // T)
    def _(i):
        at = part(i)
        products = dot(solved_ref[:, at], rest_ref[:, N:], 0, 0)
        block_ref[at, :] = high_ref[at, :] + dot(high_gen_ref[at, :], high_gen_ref[...], 1, 1) - products[:, :N]
        gen_ref[at, :] = high_gen_ref[at, :] - products[:, N:]

    own = pl.ds(pl.multiple_of(member * SHARE, 8), SHARE)
    if last:
        outs[4][...] = block_ref[own, :]
        outs[5][...] = gen_ref[own, :]
    else:
        for k, (i, j) in enumerate(LOWER):
            packed_ref[T * k : T * (k + 1), :] = block_ref[T * i : T * (i + 1), T * j : T * (j + 1)]
        packed_ref[T * len(LOWER) :, :] = gen_ref[...]
        quarter = 2 * row + (member & 1)
        outs[6][...] = packed_ref[pl.ds(pl.multiple_of(quarter * QUARTER, 8), QUARTER), :]


def merge(height, place, ranks, gathered, mixing, own):
    last = height == LEVELS - 1
    shapes = [(N, N), (N // T, T, T), (N, N), (N, N)]
    shapes += [(SHARE, N), (SHARE, K)] if last else [(N, N), (N, K), (QUARTER, T)]
    kept = [(N, N), (N, N), (N, K), (N, K), (N, N), (N, 2 * N + K), (4 * QUARTER, T)] + ([(N, N), (N, K)] if last else [])
    return pl.pallas_call(
        functools.partial(merge_kernel, height),
        out_shape=[jax.ShapeDtypeStruct(shape, jnp.float32) for shape in shapes],
        in_specs=[SMEM, SMEM] + [VMEM] * (4 + len(own)),
        out_specs=[VMEM] * len(shapes),
        scratch_shapes=[pltpu.VMEM(shape, jnp.float32) for shape in kept],
        compiler_params=pltpu.CompilerParams(vmem_limit_bytes=40 * 2**20),
        cost_estimate=pl.CostEstimate(flops=2 * 10**10, transcendentals=0, bytes_accessed=8 * 10**6),
        name="merge%d" % height,
    )(place, ranks, gathered, *mixing, *own)


def rhs_kernel(height, place, ranks, solved, inverses, above, mixing, own, peer, out):
    leaf = place[0]
    upper = leaf >> height & 1 == 1
    low = jnp.where(upper, peer[...], own[...])
    high = jnp.where(upper, own[...], peer[...])
    if height == 0:
        base = leaf >> 1 << 1
        rows = lax.broadcasted_iota(jnp.int32, low.shape, 0)
        low = jnp.where(rows < ranks[base], low, 0.0)
        high = jnp.where(rows < ranks[base + 1], high, 0.0)
    rest = low + dot(mixing[...], high, 0, 0)
    done = []
    for i in range(N // T):
        done.append(dot(inverses[i], rest[:T]))
        at = T * (i + 1)
        if at < N:
            rest = rest[T:] - dot(above[T * i : at, at:], done[-1], 0, 0)
    out[...] = high - dot(solved[...], jnp.concatenate(done, axis=0), 0, 0)


def merge_rhs(height, place, ranks, solved, inverses, above, mixing, own, peer):
    return pl.pallas_call(
        functools.partial(rhs_kernel, height),
        out_shape=jax.ShapeDtypeStruct(own.shape, jnp.float32),
        in_specs=[SMEM, SMEM] + [VMEM] * 6,
        out_specs=VMEM,
        compiler_params=pltpu.CompilerParams(vmem_limit_bytes=24 * 2**20),
        cost_estimate=pl.CostEstimate(flops=3 * 10**9, transcendentals=0, bytes_accessed=3 * 10**6),
        name="rhs%d" % height,
    )(place, ranks, solved, inverses, above, mixing, own, peer)


def swapped(block, bit):
    route = []
    for low in range(16):
        if bit < 3:
            high = low ^ 1 << bit
        else:
            high = (low + 4 if low >> 2 & 1 else low - 4) % 16
        route.append((low, high))
    return lax.ppermute(block, Z, route)


def joined(own, peer, bit):
    upper = lax.axis_index("z%d" % bit) == 1
    return jnp.where(upper, jnp.concatenate([peer, own]), jnp.concatenate([own, peer]))


def across_core(block):
    return lax.ppermute(block, "c", [(0, 1), (1, 0)])


def around_chips(block):
    routes = [[(y, (y + away) % 4) for y in range(4)] for away in (1, 3, 2)]
    first, third, second = [lax.ppermute(block, "y", route) for route in routes]
    return jnp.stack([block, first, second, third])


def across_chip(block):
    return lax.ppermute(block, "y", [(0, 1), (1, 0), (2, 3), (3, 2)])


def on_device(diag_block, generator, right_sides, *rest):
    pieces, node_ranks = rest[:LEVELS], rest[LEVELS]
    leaf = lax.axis_index(LEAF)
    member = lax.axis_index(GRP)
    core = lax.axis_index("c")
    quarter = 2 * (lax.axis_index("y") & 1) + core
    place = jnp.where(jnp.arange(2) == 0, leaf, member).astype(jnp.int32)
    third = SHARE // 3
    packed_gen = jnp.concatenate([generator[third * q : third * (q + 1)] for q in range(3)], axis=1)
    share = jnp.concatenate([diag_block, packed_gen], axis=0)
    tiles = []
    for height, piece in enumerate(pieces):
        count = piece.shape[0] // MIXED[height]
        at = (quarter if height else core) % count * MIXED[height]
        tiles.append(lax.dynamic_slice_in_dim(piece, at, MIXED[height], 0))

    def step(bit, start):
        moved = tiles[start:]
        return swapped(jnp.concatenate(moved, axis=0), bit)

    def join(received, bit, start):
        offset = 0
        for height in range(start, LEVELS):
            count = tiles[height].shape[0]
            tiles[height] = joined(tiles[height], received[offset : offset + count], bit)
            offset += count

    peer_share = swapped(share, 0)
    near = swapped(tiles[0], 0)
    moving = step(0, 1)
    peer_share, near, moving = lax.optimization_barrier((peer_share, near, moving))
    mine = around_chips(jnp.concatenate([share, peer_share], axis=0))
    mixing = (pieces[0], near, across_core(near))
    join(moving, 0, 1)
    moving = step(1, 1)
    rhs_now = right_sides
    peer_rhs = swapped(rhs_now, 0)
    gathered, own = mine, (across_core(mine),)
    for height in range(LEVELS):
        made = merge(height, place, node_ranks, gathered, mixing, own)
        factors, own = made[:4], made[4:6]
        if height == LEVELS - 1:
            rhs_now = merge_rhs(height, place, node_ranks, *factors, rhs_now, peer_rhs)
            break
        if moving is not None:
            share, peer_rhs, moving = lax.optimization_barrier((made[6], peer_rhs, moving))
        else:
            share, peer_rhs = lax.optimization_barrier((made[6], peer_rhs))
        peer_share = swapped(share, height + 1)
        if moving is not None:
            join(moving, height + 1, height + 1)
        tile = tiles[height + 1]
        near = across_chip(tile)
        mixing = (tile, near, across_core(jnp.concatenate([tile, near], axis=0)))
        rhs_now = merge_rhs(height, place, node_ranks, *factors, rhs_now, peer_rhs)
        moving = None
        if height == 1:
            moving = step(3, 3)
            peer_share, rhs_now, moving = lax.optimization_barrier((peer_share, rhs_now, moving))
            join(moving, 3, 3)
            moving = None
        else:
            peer_share, rhs_now = lax.optimization_barrier((peer_share, rhs_now))
        peer_rhs = swapped(rhs_now, height + 1)
        halves = jnp.stack([peer_share, across_chip(peer_share)])
        gathered = lax.all_gather(halves, "c", axis=0)
        if height == 0:
            gathered, *tiles[height + 2 :] = lax.optimization_barrier((gathered, *tiles[height + 2 :]))
            moving = step(height + 2, height + 2)
    return (own[0], own[1], rhs_now)


def solution(mesh):
    fine = Mesh(mesh.devices.reshape(4, 2, 2, 2, 2, 4, 2), LEAF + GRP)
    rows = P(LEAF + GRP, None)
    leaves = P(LEAF, None)
    columns = P(LEAF, GRP)
    return jax.shard_map(
        on_device,
        mesh=fine,
        in_specs=(rows, rows, columns, leaves, leaves, leaves, leaves, P()),
        out_specs=(rows, rows, columns),
        check_vma=False,
    )
```

```python
import functools

import jax
import jax.numpy as jnp
from jax import lax
from jax.experimental import pallas as pl
from jax.experimental.pallas import tpu as pltpu
from jax.sharding import Mesh, PartitionSpec as P

LEVELS = 4
N = 384
K = 128
T = 128
W = 16
SHARE = 48
PACK = 64
LOWER = ((0, 0), (1, 0), (1, 1), (2, 0), (2, 1), (2, 2))
QUARTER = (6 * T + N) // 4
LEAF = ("x", "z3", "z2", "z1", "z0")
GRP = ("y", "c")
Z = ("z3", "z2", "z1", "z0")
MIXED = (96, 24, 16, 8)
HIGHEST = lax.Precision.HIGHEST
VMEM = pl.BlockSpec(memory_space=pltpu.VMEM)
SMEM = pl.BlockSpec(memory_space=pltpu.SMEM)


def dot(first, second, first_axis=1, second_axis=0):
    return lax.dot_general(
        first,
        second,
        (((first_axis,), (second_axis,)), ((), ())),
        precision=HIGHEST,
        preferred_element_type=jnp.float32,
    )


def wide(values):
    return jnp.broadcast_to(values, (8, T))


def sweep_panel(rows, start):
    lanes = lax.broadcasted_iota(jnp.int32, (8, T), 1)
    subs = lax.broadcasted_iota(jnp.int32, (8, T), 0)
    cols = [[wide(part[:, start + m : start + m + 1]) for part in rows] for m in range(W)]
    factor = [jnp.zeros((8, T), jnp.float32) for _ in rows]
    for k in range(W):
        group, sub = divmod(k, 8)
        here = subs == sub
        pivot = wide(cols[k][group][sub : sub + 1, :])
        inverse = 1.0 / pivot
        mult = list(cols[k])
        mult[group] = jnp.where(here, -1.0, mult[group])
        for m in range(k + 1, W):
            step = wide(cols[m][group][sub : sub + 1, :]) * inverse
            kept = list(cols[m])
            kept[group] = jnp.where(here, 0.0, kept[group])
            cols[m] = [part - q * step for part, q in zip(kept, mult)]
        lane = lanes == start + k
        row = jnp.where(lane, 1.0, wide(rows[group][sub : sub + 1, :]))
        scaled = jnp.where(lanes <= start + k, row, 0.0) * lax.rsqrt(pivot)
        factor[group] = jnp.where(here, scaled, factor[group])
        step = row * inverse
        kept = [jnp.where(lane | here if i == group else lane, 0.0, part) for i, part in enumerate(rows)]
        rows = [part - q * step for part, q in zip(kept, mult)]
    return rows, factor


def inverse_factor(block):
    lanes = lax.broadcasted_iota(jnp.int32, (8, T), 1)
    rows = [block[8 * i : 8 * i + 8, :] for i in range(W // 8)]
    below = block[W:]
    out = []
    for start in range(0, T, W):
        swept, factor = sweep_panel(rows, start)
        out += factor
        if start + W == T:
            break
        panel = jnp.concatenate(swept, axis=0)
        inside = (lanes >= start) & (lanes < start + W)
        rows = []
        for i in range(W // 8):
            part = below[8 * i : 8 * i + 8, :]
            total = jnp.where(inside, 0.0, part)
            for k in range(W):
                total = total - wide(part[:, start + k : start + k + 1]) * wide(panel[k : k + 1, :])
            rows.append(total)
        if start + 2 * W < T:
            below = below[W:]
            drop = dot(below[:, start : start + W], panel)
            span = lax.broadcasted_iota(jnp.int32, below.shape, 1)
            below = jnp.where((span >= start) & (span < start + W), 0.0, below) - drop
    return jnp.concatenate(out, axis=0)


def unpack(mine, theirs, member, first):
    blocks, gens = [], []
    for y in range(4):
        away = (member >> 1) - y & 3
        here, there = mine[away, first : first + PACK, :], theirs[away, first : first + PACK, :]
        even = member & 1 == 0
        for share in (jnp.where(even, here, there), jnp.where(even, there, here)):
            blocks.append(share[:SHARE])
            gens += [share[SHARE:, K * q : K * (q + 1)] for q in range(3)]
    return jnp.concatenate(blocks, axis=0), jnp.concatenate(gens, axis=0)


def unpack_quarters(gathered, row, packed):
    for r in range(2):
        for c in range(2):
            at = QUARTER * (2 * r + c)
            packed[at : at + QUARTER, :] = gathered[c, row ^ r]
    tiles = {}
    for k, (i, j) in enumerate(LOWER):
        tiles[i, j] = packed[T * k : T * (k + 1), :]
        tiles[j, i] = tiles[i, j] if i == j else tiles[i, j].T
    block = jnp.concatenate(
        [jnp.concatenate([tiles[i, j] for j in range(3)], axis=1) for i in range(3)], axis=0
    )
    return block, packed[T * len(LOWER) :, :]


def unpack_first(upper, core, own, near, far):
    even = core == 0
    peer = [jnp.where(even, near[...], far[...]), jnp.where(even, far[...], near[...])]
    peer = jnp.concatenate(peer, axis=0)
    return jnp.concatenate([jnp.where(upper, peer, own[...]), jnp.where(upper, own[...], peer)], axis=0)


def unpack_mixing(height, row, core, own, near, far):
    count = own.shape[0]
    front, even = row == 0, core == 0
    own, near, close, apart = own[...], near[...], far[:count, :], far[count:, :]
    mine = [jnp.where(front, own, near), jnp.where(front, near, own)]
    theirs = [jnp.where(front, close, apart), jnp.where(front, apart, close)]
    parts = []
    for first, second in zip(mine, theirs):
        parts += [jnp.where(even, first, second), jnp.where(even, second, first)]
    rows = MIXED[height]
    tiles = []
    for sub in range(2 << height):
        for part in range((N >> height + 1) // rows):
            tiles.append(parts[part][sub * rows : (sub + 1) * rows, :])
    return jnp.concatenate(tiles, axis=0)


def masked(block, gen, rank):
    rows = lax.broadcasted_iota(jnp.int32, (N, N), 0)
    cols = lax.broadcasted_iota(jnp.int32, (N, N), 1)
    identity = jnp.where(rows == cols, 1.0, 0.0)
    block = jnp.where((rows < rank) & (cols < rank), block, identity)
    inside = lax.broadcasted_iota(jnp.int32, (N, K), 0) < rank
    return block, jnp.where(inside, gen, 0.0)


def merge_kernel(height, place, ranks, gathered, mixing_own, mixing_near, mixing_far, *refs):
    last = height == LEVELS - 1
    leaf, member = place[0], place[1]
    base = leaf >> height + 1 << height + 1
    low_rank = ranks[base + 2**height - 1]
    high_rank = ranks[base + 2 ** (height + 1) - 1]
    upper = leaf >> height & 1 == 1
    held = 9 if last else 7
    refs, scratch = refs[:-held], refs[-held:]
    packed_ref = scratch[6]
    row = member >> 1 & 1
    if height == 0:
        own_block, own_gen = unpack(gathered, refs[0], member, 0)
        peer_block, peer_gen = unpack(gathered, refs[0], member, PACK)
        outs = refs[1:]
        mixing = unpack_first(upper, member & 1, mixing_own, mixing_near, mixing_far)
    else:
        peer_block, peer_gen = unpack_quarters(gathered, row, packed_ref)
        own_block, own_gen = refs[0][...], refs[1][...]
        outs = refs[2:]
        mixing = unpack_mixing(height, row, member & 1, mixing_own, mixing_near, mixing_far)
    low_block = jnp.where(upper, peer_block, own_block)
    high_block = jnp.where(upper, own_block, peer_block)
    low_gen = jnp.where(upper, peer_gen, own_gen)
    high_gen = jnp.where(upper, own_gen, peer_gen)
    if height == 0:
        low_block, low_gen = masked(low_block, low_gen, low_rank)
        high_block, high_gen = masked(high_block, high_gen, high_rank)
    rows = lax.broadcasted_iota(jnp.int32, (N, N), 0)
    cols = lax.broadcasted_iota(jnp.int32, (N, N), 1)
    inside = (rows < high_rank) & (cols < low_rank)
    solved_ref, inverse_ref, above_ref, mixing_ref, block_ref, gen_ref = outs[:6]
    low_ref, high_ref, low_gen_ref, high_gen_ref, mixed_ref, rest_ref = scratch[:6]
    if last:
        block_ref, gen_ref = scratch[7:]
    mixing_ref[...] = jnp.where(inside, mixing, 0.0)
    low_ref[...], high_ref[...] = low_block, high_block
    low_gen_ref[...], high_gen_ref[...] = low_gen, high_gen

    def part(i):
        return pl.ds(pl.multiple_of(i * T, T), T)

    @pl.loop(0, N // T)
    def _(i):
        at = part(i)
        mixed_ref[at, :] = dot(high_ref[at, :], mixing_ref[...])
        rest_ref[at, 2 * N :] = low_gen_ref[at, :] + dot(mixing_ref[:, at], high_gen_ref[...], 0, 0)

    for top in range(0, N, T):
        at = slice(top, top + T)
        gen_input = rest_ref[at, 2 * N :]
        pivot = low_ref[at, top:] + dot(gen_input, rest_ref[top:, 2 * N :], 1, 1)
        rest_ref[at, top:N] = pivot + dot(mixing_ref[:, at], mixed_ref[:, top:], 0, 0)
        rest_ref[at, N : 2 * N] = dot(gen_input, high_gen_ref[...], 1, 1) + mixed_ref[:, at].T

    @pl.loop(0, N // T)
    def _(i):
        at = part(i)
        inverse = inverse_factor(rest_ref[at, at])
        inverse_ref[i] = inverse
        for step in range(N // T):

            @pl.when(i == step)
            def _():
                top, low = T * step, T * (step + 1)
                done = dot(inverse, rest_ref[top:low, low:])
                rest_ref[top:low, low:] = done
                if low < N:
                    above_ref[top:low, low:] = done[:, : N - low]
                for later in range(low, N, T):
                    from_here = done[:, later - low :]
                    rest_ref[later : later + T, later:] -= dot(from_here[:, :T], from_here, 0, 0)

    solved_ref[...] = rest_ref[:, N : 2 * N]
    for top in range(0, N, T):
        at = slice(top, top + T)
        products = dot(solved_ref[:, at], rest_ref[:, N + top :], 0, 0)
        tiles = high_ref[at, top:] + dot(high_gen_ref[at, :], high_gen_ref[top:, :], 1, 1) - products[:, : N - top]
        block_ref[at, top:] = tiles
        for later in range(top + T, N, T):
            block_ref[later : later + T, at] = tiles[:, later - top : later - top + T].T
        gen_ref[at, :] = high_gen_ref[at, :] - products[:, N - top :]

    own = pl.ds(pl.multiple_of(member * SHARE, 8), SHARE)
    if last:
        outs[4][...] = block_ref[own, :]
        outs[5][...] = gen_ref[own, :]
    else:
        for k, (i, j) in enumerate(LOWER):
            packed_ref[T * k : T * (k + 1), :] = block_ref[T * i : T * (i + 1), T * j : T * (j + 1)]
        packed_ref[T * len(LOWER) :, :] = gen_ref[...]
        quarter = 2 * row + (member & 1)
        outs[6][...] = packed_ref[pl.ds(pl.multiple_of(quarter * QUARTER, 8), QUARTER), :]


def merge(height, place, ranks, gathered, mixing, own):
    last = height == LEVELS - 1
    shapes = [(N, N), (N // T, T, T), (N, N), (N, N)]
    shapes += [(SHARE, N), (SHARE, K)] if last else [(N, N), (N, K), (QUARTER, T)]
    kept = [(N, N), (N, N), (N, K), (N, K), (N, N), (N, 2 * N + K), (4 * QUARTER, T)] + ([(N, N), (N, K)] if last else [])
    return pl.pallas_call(
        functools.partial(merge_kernel, height),
        out_shape=[jax.ShapeDtypeStruct(shape, jnp.float32) for shape in shapes],
        in_specs=[SMEM, SMEM] + [VMEM] * (4 + len(own)),
        out_specs=[VMEM] * len(shapes),
        scratch_shapes=[pltpu.VMEM(shape, jnp.float32) for shape in kept],
        compiler_params=pltpu.CompilerParams(vmem_limit_bytes=40 * 2**20),
        cost_estimate=pl.CostEstimate(flops=2 * 10**10, transcendentals=0, bytes_accessed=8 * 10**6),
        name="merge%d" % height,
    )(place, ranks, gathered, *mixing, *own)


def rhs_kernel(height, place, ranks, solved, inverses, above, mixing, own, peer, out):
    leaf = place[0]
    upper = leaf >> height & 1 == 1
    low = jnp.where(upper, peer[...], own[...])
    high = jnp.where(upper, own[...], peer[...])
    if height == 0:
        base = leaf >> 1 << 1
        rows = lax.broadcasted_iota(jnp.int32, low.shape, 0)
        low = jnp.where(rows < ranks[base], low, 0.0)
        high = jnp.where(rows < ranks[base + 1], high, 0.0)
    rest = low + dot(mixing[...], high, 0, 0)
    done = []
    for i in range(N // T):
        done.append(dot(inverses[i], rest[:T]))
        at = T * (i + 1)
        if at < N:
            rest = rest[T:] - dot(above[T * i : at, at:], done[-1], 0, 0)
    out[...] = high - dot(solved[...], jnp.concatenate(done, axis=0), 0, 0)


def merge_rhs(height, place, ranks, solved, inverses, above, mixing, own, peer):
    return pl.pallas_call(
        functools.partial(rhs_kernel, height),
        out_shape=jax.ShapeDtypeStruct(own.shape, jnp.float32),
        in_specs=[SMEM, SMEM] + [VMEM] * 6,
        out_specs=VMEM,
        compiler_params=pltpu.CompilerParams(vmem_limit_bytes=24 * 2**20),
        cost_estimate=pl.CostEstimate(flops=3 * 10**9, transcendentals=0, bytes_accessed=3 * 10**6),
        name="rhs%d" % height,
    )(place, ranks, solved, inverses, above, mixing, own, peer)


def swapped(block, bit):
    route = []
    for low in range(16):
        if bit < 3:
            high = low ^ 1 << bit
        else:
            high = (low + 4 if low >> 2 & 1 else low - 4) % 16
        route.append((low, high))
    return lax.ppermute(block, Z, route)


def joined(own, peer, bit):
    upper = lax.axis_index("z%d" % bit) == 1
    return jnp.where(upper, jnp.concatenate([peer, own]), jnp.concatenate([own, peer]))


def across_core(block):
    return lax.ppermute(block, "c", [(0, 1), (1, 0)])


def around_chips(block):
    routes = [[(y, (y + away) % 4) for y in range(4)] for away in (1, 3, 2)]
    first, third, second = [lax.ppermute(block, "y", route) for route in routes]
    return jnp.stack([block, first, second, third])


def across_chip(block):
    return lax.ppermute(block, "y", [(0, 1), (1, 0), (2, 3), (3, 2)])


def on_device(diag_block, generator, right_sides, *rest):
    pieces, node_ranks = rest[:LEVELS], rest[LEVELS]
    leaf = lax.axis_index(LEAF)
    member = lax.axis_index(GRP)
    core = lax.axis_index("c")
    quarter = 2 * (lax.axis_index("y") & 1) + core
    place = jnp.where(jnp.arange(2) == 0, leaf, member).astype(jnp.int32)
    third = SHARE // 3
    packed_gen = jnp.concatenate([generator[third * q : third * (q + 1)] for q in range(3)], axis=1)
    share = jnp.concatenate([diag_block, packed_gen], axis=0)
    tiles = []
    for height, piece in enumerate(pieces):
        count = piece.shape[0] // MIXED[height]
        at = (quarter if height else core) % count * MIXED[height]
        tiles.append(lax.dynamic_slice_in_dim(piece, at, MIXED[height], 0))

    def step(bit, start):
        moved = tiles[start:]
        return swapped(jnp.concatenate(moved, axis=0), bit)

    def join(received, bit, start):
        offset = 0
        for height in range(start, LEVELS):
            count = tiles[height].shape[0]
            tiles[height] = joined(tiles[height], received[offset : offset + count], bit)
            offset += count

    peer_share = swapped(share, 0)
    peer_share, *tiles = lax.optimization_barrier((peer_share, *tiles))
    mine = around_chips(jnp.concatenate([share, peer_share], axis=0))
    near = swapped(tiles[0], 0)
    moving = step(0, 1)
    mine, moving, near = lax.optimization_barrier((mine, moving, near))
    mixing = (pieces[0], near, across_core(near))
    join(moving, 0, 1)
    moving = step(1, 1)
    rhs_now = right_sides
    peer_rhs = swapped(rhs_now, 0)
    gathered, own = mine, (across_core(mine),)
    for height in range(LEVELS):
        made = merge(height, place, node_ranks, gathered, mixing, own)
        factors, own = made[:4], made[4:6]
        if height == LEVELS - 1:
            rhs_now = merge_rhs(height, place, node_ranks, *factors, rhs_now, peer_rhs)
            break
        if moving is not None:
            share, peer_rhs, moving = lax.optimization_barrier((made[6], peer_rhs, moving))
        else:
            share, peer_rhs = lax.optimization_barrier((made[6], peer_rhs))
        peer_share = swapped(share, height + 1)
        if moving is not None:
            join(moving, height + 1, height + 1)
        tile = tiles[height + 1]
        near = across_chip(tile)
        mixing = (tile, near, across_core(jnp.concatenate([tile, near], axis=0)))
        rhs_now = merge_rhs(height, place, node_ranks, *factors, rhs_now, peer_rhs)
        moving = None
        if height == 1:
            moving = step(3, 3)
            peer_share, rhs_now, moving = lax.optimization_barrier((peer_share, rhs_now, moving))
            join(moving, 3, 3)
            moving = None
        else:
            peer_share, rhs_now = lax.optimization_barrier((peer_share, rhs_now))
        peer_rhs = swapped(rhs_now, height + 1)
        halves = jnp.stack([peer_share, across_chip(peer_share)])
        gathered = lax.all_gather(halves, "c", axis=0)
        if height == 0:
            gathered, *tiles[height + 2 :] = lax.optimization_barrier((gathered, *tiles[height + 2 :]))
            moving = step(height + 2, height + 2)
    return (own[0], own[1], rhs_now)


def solution(mesh):
    fine = Mesh(mesh.devices.reshape(4, 2, 2, 2, 2, 4, 2), LEAF + GRP)
    rows = P(LEAF + GRP, None)
    leaves = P(LEAF, None)
    columns = P(LEAF, GRP)
    return jax.shard_map(
        on_device,
        mesh=fine,
        in_specs=(rows, rows, columns, leaves, leaves, leaves, leaves, P()),
        out_specs=(rows, rows, columns),
        check_vma=False,
    )
```
